32 devices in a mesh: pool: 4 (over y, core), expert: 8 (over z, x).
Axes of the slice: x: 2, y: 2, z: 4, core: 2. Of those that a mesh axis runs over, the one named last changes fastest.
Arguments:
- residual: bfloat16 [64, 2, 4096], P('expert'), may hold values from -6 to 6
- queries: bfloat16 [64, 2, 32, 128], P('expert', None, 'pool'), may hold values from -150 to 150
- kv_cache: bfloat16 [64, 512, 2, 2, 128], P('expert'), may hold values from -6 to 6
- kv_pages: bfloat16 [16, 8, 64, 2, 2, 128], P('pool', 'expert'), may hold values from -6 to 6
- cache_len: int32 [64], P('expert'), may hold values from 1 to 510, 16320 in all
- page_row: int32 [16, 8], P(None, 'expert'), may hold values from 0 to 7
- page_len: int32 [16, 8], P(None, 'expert'), may hold values from 1 to 64
- routes: int32 [64, 2, 8], P('expert'), may hold values from 0 to 15, all different within a row; in each aligned block of 16 rows (0 to 15, 16 to 31, ..., all dimensions but the last counted through in order) at most 12 rows name the same one
- route_weight: float32 [64, 2, 8], P('expert'), may hold values from 0.05 to 0.5
- out_weight: bfloat16 [4096, 4096], P('pool'), may hold values from -1.5 to 1.5
- gate_weight: bfloat16 [16, 4096, 1024], P('expert', None, 'pool'), may hold values from -0.09375 to 0.09375
- up_weight: bfloat16 [16, 4096, 1024], P('expert', None, 'pool'), may hold values from -0.09375 to 0.09375
- down_weight: bfloat16 [16, 1024, 4096], P('expert', 'pool'), may hold values from -0.375 to 0.375
Outputs:
- layer_out: bfloat16 [64, 2, 4096], P('expert')
The draws below stay inside these ranges and needn't reach their ends.
Inputs may be any that keep to these rules, and one draw needn't show every extreme that they name: The row's two new tokens sit at positions cache_len and cache_len + 1 of its cache. The page belongs to row e * 8 + page_row of its group e. `routes`: a token names distinct experts; among the 16 new tokens of one device's rows no expert is named by more than 12 tokens.
All inputs are finite; a program needn't handle non-finite values. No bound on the sum of `cache_len` on one device may be relied on, other than what follows from the above.
Results may differ from the reference program's by a relative error of at most 0.028.
Values may be sent and summed in bfloat16 or wider, within the bound.
No kernel may reach another device: no remote copies, remote signals or barrier semaphores. Data moves between devices by JAX's collectives and lax.ppermute only.
A program may use at most 64 MiB of HBM per device.

```python
import math
import jax
import jax.numpy as jnp
import numpy as np
from jax import lax

D = 4096
QH = 32
KVH = 2
HD = 128
FF = 1024
TOP = 8
R_DEV = 8
LMAX = 512
PAGE = 64
ROWS = 64
EXPERTS = 16
SLOTS = 16
CAP = 12
N_POOL = 4
N_EXPERT = 8


def cache_numbers(key):
    base = jax.random.truncated_normal(jax.random.fold_in(key, 11), -6.0, 6.0, (ROWS, LMAX, KVH, 2, HD), jnp.float32)
    return base


def draw_kv_cache(key, part):
    return cache_numbers(key).astype(jnp.bfloat16)


def draw_queries(key, part):
    base = jax.random.truncated_normal(jax.random.fold_in(key, 23), -6.0, 6.0, (ROWS, 2, QH, HD), jnp.float32)
    return base.astype(jnp.bfloat16)


def set_ends(drawn, rng, low, top_value):
    spot = [jax.random.randint(jax.random.fold_in(rng, axis), (), 0, length) for axis, length in enumerate(drawn.shape)]
    widest = drawn.shape.index(max(drawn.shape))
    next_to = spot[:widest] + [(spot[widest] + 1) % drawn.shape[widest]] + spot[widest + 1:]
    return drawn.at[tuple(spot)].set(low).at[tuple(next_to)].set(top_value)


def steps_of(stream_key, shape, split, least, largest):
    level = 1.0
    for dim, parts in split:
        draws = jax.random.uniform(jax.random.fold_in(jax.random.fold_in(stream_key, 6), dim), (parts,), jnp.float32, least / len(split), largest / len(split))
        level = level * jnp.repeat(jnp.exp(draws), shape[dim] // parts).reshape((-1,) + (1,) * (len(shape) - 1 - dim))
    return level


def length_profile(amount, total, most, lean):
    weights = [(1 << 20) // math.isqrt(rank ** lean) + 1 for rank in range(2, amount + 1)]
    surplus, holding = total - most - (amount - 1), [1] * (amount - 1)
    while surplus > 0:
        movable = [i for i in range(amount - 1) if holding[i] < most]
        mass, left = sum([weights[i] for i in movable]), surplus
        for i in movable:
            more = min(most - holding[i], max(1, left * weights[i] // mass), surplus)
            holding[i] = holding[i] + more
            surplus = surplus - more
    return np.array([most] + holding)


def ragged_sizes(stream_key, count, total, limit, skew):
    if count == 2:
        one = jax.random.randint(stream_key, (), max(1, total - limit), min(limit, total - 1) + 1)
        return jnp.stack([one, total - one])
    tallies = jnp.asarray(length_profile(count, total, limit, skew), jnp.int32)
    couples = (count - 1) // 2
    giver, taker = tallies[1:1 + 2 * couples:2], tallies[2:2 + 2 * couples:2]
    room = jnp.minimum(giver - 1, limit - taker)
    moved = jax.random.randint(jax.random.fold_in(stream_key, 1), (couples,), 0, 1 << 20) % (room + 1)
    tallies = tallies.at[1:1 + 2 * couples:2].set(giver - moved).at[2:2 + 2 * couples:2].set(taker + moved)
    return tallies[jax.random.permutation(jax.random.fold_in(stream_key, 2), count)]


def shared_out(key, own, number, rows, count, top, bound, slope):
    order = jax.random.permutation(key, count)
    packed, common = portions_of(count, rows * top, bound, slope, True), portions_of(count, rows * top, bound, slope, False)
    places = jnp.arange(count)

    def named(sizes, rotation):
        used = int((sizes > 0).sum())
        fixed = max(1, used // 4)
        passed = fixed + (places - fixed + rotation * (used - fixed)) % max(1, count - fixed)
        return jnp.zeros((count,), jnp.int32).at[order[jnp.where(places < fixed, places, passed)]].set(jnp.asarray(sizes, jnp.int32))

    sizes = jnp.where(number % 4 == 0, named(packed, number // 4), named(common, number - number // 4 - 1))
    mixed = jax.random.permutation(jax.random.fold_in(own, 3), count)
    donor, taker = mixed[0:count // 2 * 2:2], mixed[1:count // 2 * 2:2]
    margin = jnp.minimum(sizes[donor] - 1, bound - sizes[taker]) // 2
    margin = jnp.where((donor == order[0]) | (taker == order[0]) | (sizes[taker] == 0), 0, jnp.maximum(margin, 0))
    passed = jax.random.randint(jax.random.fold_in(own, 4), (count // 2,), 0, 1 << 20) % (margin + 1)
    sizes = sizes.at[donor].add(-passed).at[taker].add(passed)
    labels = jnp.searchsorted(jnp.cumsum(sizes), jnp.arange(rows * top), side="right").astype(jnp.int32)
    table = labels.reshape(top, rows).T
    table = table[jax.random.permutation(jax.random.fold_in(own, 1), rows)]
    rotation = jax.random.randint(jax.random.fold_in(own, 2), (rows, 1), 0, top)
    return jnp.take_along_axis(table, (jnp.arange(top)[None, :] + rotation) % top, axis=1)


def portions_of(count, total, most, skew, full):
    weights = [(1 << 20) // math.isqrt(standing ** skew) + 1 for standing in range(1, count + 1)]
    largest = most if full else min(most, max(-(-total // count), total * weights[0] // sum(weights)))
    least = 1 if total - largest >= count - 1 else 0
    counts, surplus = [largest] + [least] * (count - 1), total - largest - least * (count - 1)
    while surplus > 0:
        movable = [i for i in range(1, count) if counts[i] < largest] or [i for i in range(1, count) if counts[i] < most]
        pool, remaining = sum([weights[i] for i in movable]), surplus
        for i in movable:
            extra = min(most - counts[i], max(1, remaining * weights[i] // pool), surplus)
            counts[i] = counts[i] + extra
            surplus = surplus - extra
    return np.array(counts)


def normal_values(key, extent, width, reach, shards=(), kind=jnp.bfloat16):
    values = width * jax.random.normal(key, extent, jnp.float32)
    if shards:
        values = values * steps_of(key, extent, shards, -0.22, 0.18)
    return jnp.clip(values, -reach, reach).astype(kind)


def setup_inputs(seed: int = 0) -> dict:
    key_list = jax.random.split(jax.random.key(seed), 14)
    residual = normal_values(key_list[0], (ROWS, 2, D), 1.0, 6.0, ((0, 8),))
    queries = draw_queries(jax.random.fold_in(key_list[13], 71), 0)
    kv_cache = draw_kv_cache(jax.random.fold_in(key_list[13], 71), 0)
    kv_pages = normal_values(key_list[3], (SLOTS, N_EXPERT, PAGE, KVH, 2, HD), 1.0, 6.0, ((0, 4), (1, 8)))
    cache_len = ragged_sizes(key_list[4], ROWS, ROWS * (LMAX - 2) // 2, LMAX - 2, 2).astype(jnp.int32)
    page_row = set_ends(jax.random.randint(key_list[5], (SLOTS, N_EXPERT), 0, R_DEV), jax.random.fold_in(key_list[5], 1), 0, R_DEV - 1).astype(jnp.int32)
    page_len = set_ends(jax.random.randint(key_list[6], (SLOTS, N_EXPERT), 1, PAGE + 1), jax.random.fold_in(key_list[6], 1), 1, PAGE).astype(jnp.int32)
    routes_keys = jax.random.split(jax.random.fold_in(key_list[7], 1), ROWS * 2 // (2 * R_DEV))
    routes_turns = jax.random.permutation(jax.random.fold_in(key_list[7], 3), ROWS * 2 // (2 * R_DEV))
    routes = jax.vmap(lambda own, number: shared_out(jax.random.fold_in(key_list[7], 2), own, number, 2 * R_DEV, EXPERTS, TOP, CAP, 2))(routes_keys, routes_turns).reshape((ROWS, 2, TOP))
    route_weight = jnp.clip(jnp.exp(math.log(0.5) - 2.3025851 * jax.random.uniform(key_list[8], (ROWS, 2, TOP), jnp.float32) ** steps_of(key_list[8], (ROWS, 2, TOP), ((0, 8),), -0.2, 0.2)), 0.05, 0.5)
    out_weight = normal_values(key_list[9], (QH * HD, D), 16 ** -0.5, 1.5, ((0, 4),))
    gate_weight = normal_values(key_list[10], (EXPERTS, D, FF), D ** -0.5, 0.09375, ((0, 8), (2, 4)))
    up_weight = normal_values(key_list[11], (EXPERTS, D, FF), D ** -0.5, 0.09375, ((0, 8), (2, 4)))
    down_weight = normal_values(key_list[12], (EXPERTS, FF, D), (FF // 4) ** -0.5, 0.375, ((0, 8), (1, 4)))
    return {"residual": residual, "queries": queries, "kv_cache": kv_cache, "kv_pages": kv_pages, "cache_len": cache_len, "page_row": page_row, "page_len": page_len, "routes": routes, "route_weight": route_weight, "out_weight": out_weight, "gate_weight": gate_weight, "up_weight": up_weight, "down_weight": down_weight}


def attend_group(operands):
    group_queries, group_cache, group_lens, group_pages, group_rows, group_sizes = operands
    heads_per = QH // KVH
    score_scale = 1.0 / (HD ** 0.5)
    grouped = group_queries.astype(jnp.float32).reshape(R_DEV, 2, KVH, heads_per, HD)
    cache_keys = group_cache[:, :, :, 0].astype(jnp.float32)
    cache_values = group_cache[:, :, :, 1].astype(jnp.float32)
    page_keys = group_pages[:, :, :, 0].astype(jnp.float32).reshape(SLOTS * PAGE, KVH, HD)
    page_values = group_pages[:, :, :, 1].astype(jnp.float32).reshape(SLOTS * PAGE, KVH, HD)
    cache_scores = jnp.einsum("rtgjd,rlgd->rtgjl", grouped, cache_keys) * score_scale
    page_scores = jnp.einsum("rtgjd,kgd->rtgjk", grouped, page_keys) * score_scale
    last_seen = group_lens[:, None] + jnp.arange(2, dtype=jnp.int32)[None, :]
    cache_allowed = (jnp.arange(LMAX, dtype=jnp.int32)[None, None, :] <= last_seen[:, :, None])[:, :, None, None, :]
    token_allowed = jnp.arange(PAGE, dtype=jnp.int32)[None, :] < group_sizes[:, None]
    page_allowed = (group_rows[None, :, None] == jnp.arange(R_DEV, dtype=jnp.int32)[:, None, None]) & token_allowed[None]
    page_allowed = page_allowed.reshape(R_DEV, 1, 1, 1, SLOTS * PAGE)
    scores = jnp.concatenate([cache_scores, page_scores], axis=-1)
    allowed = jnp.concatenate([jnp.broadcast_to(cache_allowed, cache_scores.shape), jnp.broadcast_to(page_allowed, page_scores.shape)], axis=-1)
    row_top = jnp.max(jnp.where(allowed, scores, -1e30), axis=-1, keepdims=True)
    weights = jnp.where(allowed, jnp.exp(scores - row_top), 0.0)
    row_total = jnp.sum(weights, axis=-1)
    rounded = lax.optimization_barrier(weights.astype(jnp.bfloat16)).astype(jnp.float32)
    mixed_sum = jnp.einsum("rtgjl,rlgd->rtgjd", rounded[..., :LMAX], cache_values)
    mixed_sum = mixed_sum + jnp.einsum("rtgjk,kgd->rtgjd", rounded[..., LMAX:], page_values)
    attended = mixed_sum / row_total[..., None]
    return attended.reshape(R_DEV, 2, QH * HD).astype(jnp.bfloat16)


def reference(residual, queries, kv_cache, kv_pages, cache_len, page_row, page_len, routes, route_weight, out_weight, gate_weight, up_weight, down_weight):
    operands = (
        queries.reshape(N_EXPERT, R_DEV, 2, QH, HD),
        kv_cache.reshape(N_EXPERT, R_DEV, LMAX, KVH, 2, HD),
        cache_len.reshape(N_EXPERT, R_DEV),
        jnp.moveaxis(kv_pages, 1, 0),
        page_row.T,
        page_len.T,
    )
    attended = lax.map(attend_group, operands).reshape(ROWS * 2, QH * HD)
    projected = jnp.dot(attended, out_weight, preferred_element_type=jnp.float32)
    hidden = residual.reshape(ROWS * 2, D).astype(jnp.float32) + projected
    hidden_low = hidden.astype(jnp.bfloat16)
    flat_routes = routes.reshape(ROWS * 2, TOP)
    flat_weight = route_weight.reshape(ROWS * 2, TOP)
    capacity = CAP * N_EXPERT

    def expert_rows(expert_index):
        named = flat_routes == expert_index
        chosen = jnp.any(named, axis=1)
        weight = jnp.sum(jnp.where(named, flat_weight, 0.0), axis=1)
        members = jnp.nonzero(chosen, size=capacity, fill_value=0)[0].astype(jnp.int32)
        filled = jnp.arange(capacity, dtype=jnp.int32) < jnp.sum(chosen.astype(jnp.int32))
        inputs = hidden_low[members]
        gate_value = jnp.dot(inputs, gate_weight[expert_index], preferred_element_type=jnp.float32)
        up_value = jnp.dot(inputs, up_weight[expert_index], preferred_element_type=jnp.float32)
        active = (jax.nn.silu(gate_value) * up_value).astype(jnp.bfloat16)
        sliced = active.astype(jnp.float32).reshape(capacity, N_POOL, FF // N_POOL)
        down_slices = down_weight[expert_index].astype(jnp.float32).reshape(N_POOL, FF // N_POOL, D)
        partial_value = jnp.einsum("mpf,pfd->mpd", sliced, down_slices)
        pieces = lax.optimization_barrier(partial_value.astype(jnp.bfloat16)).astype(jnp.float32)
        summed = jnp.sum(pieces, axis=1)
        factor = jnp.where(filled, weight[members], 0.0)
        return members, summed * factor[:, None]

    members, contribution = lax.map(expert_rows, jnp.arange(EXPERTS, dtype=jnp.int32))
    expert_sum = jnp.zeros((ROWS * 2, D), jnp.float32).at[members.reshape(-1)].add(contribution.reshape(-1, D))
    return (hidden + expert_sum).astype(jnp.bfloat16).reshape(ROWS, 2, D)
```

```python
import functools
import math

import jax
import jax.numpy as jnp
from jax import lax
from jax.experimental import pallas as pl
from jax.experimental.pallas import tpu as pltpu
from jax.sharding import PartitionSpec as P

MIB = 1 << 20
LANES = 128
very_low = -1e30
VMEM = pl.BlockSpec(memory_space=pltpu.VMEM)
SMEM = pl.BlockSpec(memory_space=pltpu.SMEM)
float32 = jnp.float32
bfloat16 = jnp.bfloat16


def dot_t(a, b):
    return lax.dot_general(a, b, (((1,), (1,)), ((), ())), preferred_element_type=float32)


def dot(a, b):
    return jnp.dot(a, b, preferred_element_type=float32)


def cache_kernel(heads, kv_heads, scale, head_ref, len_ref, q_ref, kv_ref, acc_ref, top_ref, total_ref):
    row = pl.program_id(0)
    kv = kv_ref[0]
    scores = dot_t(q_ref[0], kv) * scale
    lane = lax.broadcasted_iota(jnp.int32, scores.shape, 1)
    token = lax.broadcasted_iota(jnp.int32, scores.shape, 0) // heads
    wide = 2 * kv_heads
    seen = (lane // wide <= len_ref[row] + token) & (lane % wide == 2 * head_ref[0])
    scores = jnp.where(seen, scores, very_low)
    top = jnp.max(scores, axis=1, keepdims=True)
    weights = jnp.where(seen, jnp.exp(scores - top), 0.0)
    total = jnp.sum(weights, axis=1, keepdims=True)
    shifted = pltpu.roll(weights, 1, 1).astype(bfloat16)
    acc_ref[0] = dot(shifted, kv)
    top_ref[0] = jnp.broadcast_to(top, top_ref.shape[1:])
    total_ref[0] = jnp.broadcast_to(total, total_ref.shape[1:])


def page_kernel(
    heads, steps, page_size, scale, count, info_ref, page_row_ref, page_len_ref, q_ref, acc_ref, top_ref, total_ref, *rest
):
    pages = rest[:count]
    weight_ref, low_ref, send_ref, flat_ref = rest[count:]
    q = q_ref[...]
    rows = q.shape[0]
    span = 2 * page_size
    parts, allowed = [], []
    owner = lax.broadcasted_iota(jnp.int32, (rows, span), 0) // (heads * steps)
    lane = lax.broadcasted_iota(jnp.int32, (rows, span), 1)
    keys = jnp.where(lane % 2 == 0, lane // 2, page_size)
    for n in range(count):
        part = dot_t(q, pages[n][...]) * scale
        here = part.shape[1] // span
        for i in range(here):
            page = info_ref[1 + n] * here + i
            ok = (owner == page_row_ref[page, 0]) & (keys < page_len_ref[page, 0])
            allowed.append(ok)
            parts.append(jnp.where(ok, part[:, i * span : (i + 1) * span], very_low))
    scores = jnp.concatenate(parts, axis=1)
    seen = jnp.concatenate(allowed, axis=1)
    cache_top = top_ref[...]
    page_top = jnp.max(scores, axis=1, keepdims=True)
    top = jnp.maximum(cache_top, page_top)
    weights = jnp.where(seen, jnp.exp(scores - top[:, :1]), 0.0)
    shrink = jnp.exp(cache_top - top)
    total = total_ref[...] * shrink + jnp.sum(weights, axis=1, keepdims=True)
    shifted = pltpu.roll(weights, 1, 1).astype(bfloat16)
    mixed = acc_ref[...] * shrink
    size = shifted.shape[1] // count
    for n in range(count):
        mixed = mixed + dot(shifted[:, n * size : (n + 1) * size], pages[n][...])
    flat_ref[...] = mixed / total
    tokens = rows // heads
    low = jnp.concatenate(
        [flat_ref[pl.ds(h, tokens, stride=heads), :].astype(bfloat16) for h in range(heads)], axis=1
    )
    low_ref[...] = low
    half = send_ref.shape[1]
    start = pl.multiple_of((1 - info_ref[0]) * half, half)
    send_ref[...] = dot(low, weight_ref[:, pl.ds(start, half)]).astype(bfloat16)


def project_kernel(core_ref, low_ref, weight_ref, keep_ref):
    half = keep_ref.shape[1]
    start = pl.multiple_of(core_ref[0] * half, half)
    keep_ref[...] = dot(low_ref[...], weight_ref[:, pl.ds(start, half)])


def expert_kernel(count, info_ref, *rest):
    own, other = rest[:count], rest[count : 2 * count]
    gate_ref, up_ref, down_ref, act_ref, send_ref = rest[2 * count :]
    half = send_ref.shape[1]
    own_all = jnp.concatenate([r[...] for r in own], axis=0)
    other_all = jnp.concatenate([r[:, :half] for r in other], axis=0)
    table = own_all[:, half:].astype(float32)
    own_all = own_all[:, :half]
    lane = lax.broadcasted_iota(jnp.int32, table.shape, 1)
    core = info_ref[0]
    first = pl.ds(pl.multiple_of(core * half, half), half)
    second = pl.ds(pl.multiple_of((1 - core) * half, half), half)
    experts, _, units = gate_ref.shape
    everyone = info_ref[2]
    for j in range(experts):
        mine = info_ref[1] * experts + j
        weight = jnp.sum(
            jnp.where((lane == mine) | (lane == mine + everyone), table, 0.0), axis=1, keepdims=True
        )
        gate = dot(own_all, gate_ref[j, first, :]) + dot(other_all, gate_ref[j, second, :])
        up = dot(own_all, up_ref[j, first, :]) + dot(other_all, up_ref[j, second, :])
        active = gate / (1.0 + jnp.exp(-gate)) * up
        act_ref[:, j * units : (j + 1) * units] = (active * weight).astype(bfloat16)
    total = 0.0
    for j in range(experts):
        total = total + dot(act_ref[:, j * units : (j + 1) * units], down_ref[j, :, second])
    send_ref[...] = total.astype(bfloat16)


def down_kernel(info_ref, act_ref, down_ref, keep_ref):
    half = keep_ref.shape[1]
    experts, units, _ = down_ref.shape
    first = pl.ds(pl.multiple_of(info_ref[0] * half, half), half)
    total = 0.0
    for j in range(experts):
        total = total + dot(act_ref[:, j * units : (j + 1) * units], down_ref[j, :, first])
    keep_ref[...] = total.astype(bfloat16)


def call(kernel, outs, specs, scratch=(), vmem=16, flops=0, bytes_accessed=0, **kw):
    return pl.pallas_call(
        kernel,
        out_shape=outs,
        in_specs=specs,
        out_specs=jax.tree.map(lambda _: VMEM, outs),
        scratch_shapes=scratch,
        compiler_params=pltpu.CompilerParams(vmem_limit_bytes=vmem * MIB),
        cost_estimate=pl.CostEstimate(flops=flops, bytes_accessed=bytes_accessed, transcendentals=0),
        **kw,
    )


def per_device(
    residual,
    queries,
    kv_cache,
    kv_pages,
    cache_len,
    page_row,
    page_len,
    routes,
    route_weight,
    out_weight,
    gate_weight,
    up_weight,
    down_weight,
):
    pool_size = lax.axis_size("pool")
    expert_size = lax.axis_size("expert")
    pool_index = lax.axis_index("pool")
    expert_index = lax.axis_index("expert")
    cores, near = 2, 2
    outer, far = pool_size // cores, expert_size // near
    core = pool_index % cores

    def swap(value, pool_flip=0, expert_flip=0):
        pairs = []
        for p in range(pool_size):
            for e in range(expert_size):
                pairs.append((p * expert_size + e, (p ^ pool_flip) * expert_size + (e ^ expert_flip)))
        return lax.ppermute(value, ("pool", "expert"), pairs)

    rows, steps, heads, head_dim = queries.shape
    length, kv_heads = kv_cache.shape[1:3]
    held, _, page_size = kv_pages.shape[:3]
    width = residual.shape[2]
    half = width // cores
    tokens = rows * steps
    scale = 1.0 / math.sqrt(head_dim)

    def head_of(pool):
        return pool * kv_heads // pool_size

    def pages_for(pool):
        picked = lax.dynamic_index_in_dim(kv_pages[:, 0], head_of(pool), 2, keepdims=False)
        return picked.reshape(held * page_size * 2, head_dim)

    my_head = head_of(pool_index)
    own_pages = pages_for(pool_index)
    sets, sources = [own_pages], [pool_index]
    for k in range(1, outer):
        flip = k * cores
        sets.append(swap(pages_for(pool_index ^ flip), flip))
        sources.append(pool_index ^ flip)
    for n in range(outer):
        sets.append(swap(sets[n], 1))
        sources.append(sources[n] ^ 1)

    group = steps * heads
    q_rows = queries.reshape(rows, group, head_dim)
    deep = length * kv_heads * 2
    kv_rows = kv_cache.reshape(rows, deep, head_dim)
    stat = jax.ShapeDtypeStruct((rows, group, head_dim), float32)
    block = lambda n: pl.BlockSpec((1, n, head_dim), lambda r: (r, 0, 0))
    acc, top, total = pl.pallas_call(
        functools.partial(cache_kernel, heads, kv_heads, scale),
        out_shape=(stat, stat, stat),
        grid=(rows,),
        in_specs=[SMEM, SMEM, block(group), block(deep)],
        out_specs=(block(group),) * 3,
        compiler_params=pltpu.CompilerParams(vmem_limit_bytes=8 * MIB),
        cost_estimate=pl.CostEstimate(
            flops=4 * rows * group * deep * head_dim, bytes_accessed=kv_cache.size * 2, transcendentals=rows * group * deep
        ),
    )(my_head[None], cache_len, q_rows, kv_rows)

    flat = lambda a: a.reshape(rows * group, head_dim)
    info = jnp.stack([core] + sources)
    low, send = call(
        functools.partial(page_kernel, heads, steps, page_size, scale, pool_size),
        (
            jax.ShapeDtypeStruct((tokens, heads * head_dim), bfloat16),
            jax.ShapeDtypeStruct((tokens, half), bfloat16),
        ),
        [SMEM] * 3 + [VMEM] * (4 + pool_size + 1),
        scratch=[pltpu.VMEM((rows * group, head_dim), float32)],
        flops=2 * tokens * heads * head_dim * half,
    )(info, page_row, page_len, flat(q_rows), flat(acc), flat(top), flat(total), *sets, out_weight)
    arrived = swap(send, 1)
    keep = call(
        project_kernel, jax.ShapeDtypeStruct((tokens, half), float32), [SMEM, VMEM, VMEM],
        flops=2 * tokens * heads * head_dim * half,
    )(core[None], low, out_weight)

    experts = gate_weight.shape[0] * expert_size
    wide = -(-2 * experts // LANES) * LANES
    routes = routes.reshape(tokens, -1)
    named = routes[:, :, None] == jnp.arange(wide, dtype=jnp.int32) % experts
    table = jnp.sum(jnp.where(named, route_weight.reshape(tokens, -1, 1), 0.0), axis=1)
    coarse = lax.reduce_precision(table, 8, 7)
    table = jnp.where(jnp.arange(wide) < experts, coarse, jnp.where(jnp.arange(wide) < 2 * experts, table - coarse, 0.0))

    own_residual = lax.dynamic_slice_in_dim(residual.reshape(tokens, width), core * half, half, 1).astype(float32)
    first = pool_index // cores == 0
    partial = keep + arrived.astype(float32) + jnp.where(first, own_residual, 0.0)
    message = jnp.concatenate([partial, table], axis=1).astype(bfloat16)

    got = {(0, 0): message}
    for e in range(near):
        for k in range(outer):
            if k or e:
                got[k, e] = swap(message, k * cores, e)
    hiddens = []
    for e in range(near):
        total = got[0, e][:, :half].astype(float32)
        for k in range(1, outer):
            total = total + got[k, e][:, :half].astype(float32)
        hiddens.append(total)
    block_low = jnp.concatenate(
        [jnp.concatenate([hiddens[e].astype(bfloat16), got[0, e][:, half:]], axis=1) for e in range(near)], axis=0
    )
    blocks = [block_low] + [swap(block_low, 0, k * near) for k in range(1, far)]
    others = [swap(b, 1) for b in blocks]

    everyone = tokens * near * far
    units = gate_weight.shape[0] * gate_weight.shape[2]
    expert_info = jnp.stack([core, expert_index, jnp.int32(experts)])
    act, outgoing = call(
        functools.partial(expert_kernel, far),
        (
            jax.ShapeDtypeStruct((everyone, units), bfloat16),
            jax.ShapeDtypeStruct((everyone, half), bfloat16),
        ),
        [SMEM] + [VMEM] * (2 * far + 3),
        vmem=24,
        flops=4 * everyone * width * units,
    )(expert_info, *blocks, *others, gate_weight, up_weight, down_weight)
    incoming = swap(outgoing, 1)
    kept = call(
        down_kernel, jax.ShapeDtypeStruct((everyone, half), bfloat16), [SMEM, VMEM, VMEM], vmem=16,
        flops=2 * everyone * half * units,
    )(expert_info, act, down_weight)
    summed = (kept.astype(float32) + incoming.astype(float32)).reshape(far, near * tokens, half)
    back = summed[0]
    for k in range(1, far):
        back = back + swap(summed[k].astype(bfloat16), 0, k * near).astype(float32)
    back = back.reshape(near, tokens, half)
    result = back[0] + hiddens[0]
    for e in range(near):
        for k in range(outer):
            if k or e:
                result = result + swap(back[e].astype(bfloat16), k * cores, e).astype(float32)
    mine = result.astype(bfloat16)
    theirs = swap(mine, 1)
    output = jnp.where(
        core == 0, jnp.concatenate([mine, theirs], axis=1), jnp.concatenate([theirs, mine], axis=1)
    )
    return output.reshape(rows, steps, width)


def solution(mesh):
    return jax.shard_map(
        per_device,
        mesh=mesh,
        in_specs=(
            P("expert", None, None),
            P("expert", None, "pool", None),
            P("expert", None, None, None, None),
            P("pool", "expert", None, None, None, None),
            P("expert"),
            P(None, "expert"),
            P(None, "expert"),
            P("expert", None, None),
            P("expert", None, None),
            P("pool", None),
            P("expert", None, "pool"),
            P("expert", None, "pool"),
            P("expert", "pool", None),
        ),
        out_specs=P("expert", None, None),
        check_vma=False,
    )
```

```python
import functools
import math

import jax
import jax.numpy as jnp
from jax import lax
from jax.experimental import pallas as pl
from jax.experimental.pallas import tpu as pltpu
from jax.sharding import PartitionSpec as P

MIB = 1 << 20
LANES = 128
very_low = -1e30
VMEM = pl.BlockSpec(memory_space=pltpu.VMEM)
SMEM = pl.BlockSpec(memory_space=pltpu.SMEM)
HBM = pl.BlockSpec(memory_space=pltpu.HBM)
ANY = pl.BlockSpec(memory_space=pl.ANY)
float32 = jnp.float32
bfloat16 = jnp.bfloat16


def far_off(array):
    return pltpu.with_memory_space_constraint(array, pltpu.HBM)


def dot_t(a, b):
    return lax.dot_general(a, b, (((1,), (1,)), ((), ())), preferred_element_type=float32)


def dot(a, b):
    return jnp.dot(a, b, preferred_element_type=float32)


def add_pages(scale, group, sets, first_pages, row_ref, len_ref, q_ref, acc_ref, top_ref, total_ref):
    parts = []
    for pages, first in zip(sets, first_pages):
        held, span = len_ref.shape[0] // first[1], None
        span = pages.shape[0] // held
        for i in range(held):
            page = first[0] * held + i
            rows = pl.ds(pl.multiple_of(row_ref[page] * group, group), group)
            kv = pages[i * span : (i + 1) * span, :]
            scores = dot_t(q_ref[rows, :], kv) * scale
            lane = lax.broadcasted_iota(jnp.int32, scores.shape, 1)
            seen = (lane // 2 < len_ref[page]) & (lane % 2 == 0)
            scores = jnp.where(seen, scores, very_low)
            top = jnp.max(scores, axis=1, keepdims=True)
            weights = jnp.where(seen, jnp.exp(scores - top), 0.0)
            total = jnp.sum(weights, axis=1, keepdims=True)
            acc = dot(pltpu.roll(weights, 1, 1).astype(bfloat16), kv)
            parts.append((rows, top, total, acc))
    before = top_ref[...]
    for rows, top, _, _ in parts:
        top_ref[rows, :] = jnp.maximum(top_ref[rows, :], top)
    shrink = jnp.exp(before - top_ref[...])
    acc_ref[...] = acc_ref[...] * shrink
    total_ref[...] = total_ref[...] * shrink
    for rows, top, total, acc in parts:
        factor = jnp.exp(top - top_ref[rows, :])
        acc_ref[rows, :] += acc * factor
        total_ref[rows, :] += total * factor


def cache_kernel(
    heads, kv_heads, pool_size, scale, info_ref, len_ref, row_ref, size_ref, q_hbm, own_ref, kv_hbm, weight_hbm, residual_hbm,
    acc_ref, top_ref, total_ref, send_ref, keep_ref, residual_ref, kv_ref, q_ref, kv_sem, weight_sem, q_sem,
):
    rows = kv_hbm.shape[0]
    q_copy = pltpu.make_async_copy(q_hbm, q_ref, q_sem.at[0])
    q_copy.start()
    copies = [pltpu.make_async_copy(kv_hbm.at[r], kv_ref.at[r], kv_sem.at[r]) for r in range(rows)]
    for copy in copies:
        copy.start()
    chunks = weight_sem.shape[1]
    deep = weight_hbm.shape[0] // chunks
    half = send_ref.shape[1]
    weights_in = []
    for side, target in enumerate((send_ref, keep_ref)):
        which = info_ref[0] if side else 1 - info_ref[0]
        columns = pl.ds(pl.multiple_of(which * half, half), half)
        for n in range(chunks):
            part = pl.ds(n * deep, deep)
            weights_in.append(
                pltpu.make_async_copy(weight_hbm.at[part, columns], target.at[part], weight_sem.at[side, n])
            )
    mine = pl.ds(pl.multiple_of(info_ref[0] * half, half), half)
    weights_in.append(pltpu.make_async_copy(residual_hbm.at[:, mine], residual_ref, q_sem.at[1]))
    for copy in weights_in:
        copy.start()
    q_copy.wait()
    group = q_ref.shape[0] // rows
    wide = 2 * kv_heads
    for r in range(rows):
        copies[r].wait()
        kv = kv_ref[r]
        here = slice(r * group, (r + 1) * group)
        scores = dot_t(q_ref[here, :], kv) * scale
        lane = lax.broadcasted_iota(jnp.int32, scores.shape, 1)
        token = lax.broadcasted_iota(jnp.int32, scores.shape, 0) // heads
        seen = (lane // wide <= len_ref[r] + token) & (lane % wide == 2 * info_ref[4])
        scores = jnp.where(seen, scores, very_low)
        top = jnp.max(scores, axis=1, keepdims=True)
        weights = jnp.where(seen, jnp.exp(scores - top), 0.0)
        total = jnp.sum(weights, axis=1, keepdims=True)
        acc_ref[here, :] = dot(pltpu.roll(weights, 1, 1).astype(bfloat16), kv)
        top_ref[here, :] = jnp.broadcast_to(top, (group, top_ref.shape[1]))
        total_ref[here, :] = jnp.broadcast_to(total, (group, total_ref.shape[1]))
    add_pages(
        scale, group, [own_ref], [(info_ref[5], pool_size)], row_ref, size_ref, q_ref, acc_ref, top_ref, total_ref
    )
    for copy in weights_in:
        copy.wait()


def page_kernel(
    heads, group, pool_size, scale, info_ref, row_ref, size_ref, q_ref, acc_in, top_in, total_in, *rest
):
    count = pool_size - 1
    pages = rest[:count]
    weight_ref, low_ref, send_ref, acc_ref, top_ref, total_ref = rest[count:]
    acc_ref[...] = acc_in[...]
    top_ref[...] = top_in[...]
    total_ref[...] = total_in[...]
    firsts = [(info_ref[6 + n], pool_size) for n in range(count)]
    add_pages(scale, group, pages, firsts, row_ref, size_ref, q_ref, acc_ref, top_ref, total_ref)
    acc_ref[...] = acc_ref[...] / total_ref[...]
    tokens = acc_ref.shape[0] // heads
    low = jnp.concatenate(
        [acc_ref[pl.ds(h, tokens, stride=heads), :].astype(bfloat16) for h in range(heads)], axis=1
    )
    low_ref[...] = low
    send_ref[...] = dot(low, weight_ref[...]).astype(bfloat16)


def load_kernel(count, *refs):
    sources, dests, sems = refs[1 : 1 + count], refs[1 + count : 1 + 2 * count], refs[-1]
    chunks = sems.shape[1]
    copies = []
    for n in range(count):
        for j in range(sources[n].shape[0]):
            size = sources[n].shape[1] // chunks
            for i in range(chunks):
                part = pl.ds(i * size, size)
                copies.append(
                    pltpu.make_async_copy(sources[n].at[j, part], dests[n].at[j, part], sems.at[n, i, j])
                )
    for copy in copies:
        copy.start()
    for copy in copies:
        copy.wait()


def project_kernel(info_ref, low_ref, weight_ref, residual_ref, keep_ref):
    first = info_ref[1].astype(float32)
    keep_ref[...] = dot(low_ref[...], weight_ref[...]) + residual_ref[...].astype(float32) * first


def expert_kernel(count, info_ref, *rest):
    own, other = rest[:count], rest[count : 2 * count]
    gate_ref, up_ref, down_ref, act_ref, send_ref = rest[2 * count :]
    half = send_ref.shape[1]
    own_all = jnp.concatenate([r[...] for r in own], axis=0)
    other_all = jnp.concatenate([r[:, :half] for r in other], axis=0)
    table = own_all[:, half:].astype(float32)
    own_all = own_all[:, :half]
    lane = lax.broadcasted_iota(jnp.int32, table.shape, 1)
    core = info_ref[0]
    first = pl.ds(pl.multiple_of(core * half, half), half)
    second = pl.ds(pl.multiple_of((1 - core) * half, half), half)
    experts, _, units = gate_ref.shape
    everyone = info_ref[3]
    for j in range(experts):
        mine = info_ref[2] * experts + j
        weight = jnp.sum(
            jnp.where((lane == mine) | (lane == mine + everyone), table, 0.0), axis=1, keepdims=True
        )
        gate = dot(own_all, gate_ref[j, first, :]) + dot(other_all, gate_ref[j, second, :])
        up = dot(own_all, up_ref[j, first, :]) + dot(other_all, up_ref[j, second, :])
        active = gate / (1.0 + jnp.exp(-gate)) * up
        act_ref[:, j * units : (j + 1) * units] = (active * weight).astype(bfloat16)
    total = 0.0
    for j in range(experts):
        total = total + dot(act_ref[:, j * units : (j + 1) * units], down_ref[j, :, second])
    send_ref[...] = total.astype(bfloat16)


def down_kernel(info_ref, act_ref, down_ref, keep_ref):
    half = keep_ref.shape[1]
    experts, units, _ = down_ref.shape
    first = pl.ds(pl.multiple_of(info_ref[0] * half, half), half)
    total = 0.0
    for j in range(experts):
        total = total + dot(act_ref[:, j * units : (j + 1) * units], down_ref[j, :, first])
    keep_ref[...] = total.astype(bfloat16)


def call(kernel, outs, specs, scratch=(), vmem=16, flops=0, bytes_accessed=0, **kw):
    return pl.pallas_call(
        kernel,
        out_shape=outs,
        in_specs=specs,
        out_specs=jax.tree.map(lambda _: VMEM, outs),
        scratch_shapes=scratch,
        compiler_params=pltpu.CompilerParams(vmem_limit_bytes=vmem * MIB),
        cost_estimate=pl.CostEstimate(flops=flops, bytes_accessed=bytes_accessed, transcendentals=0),
        **kw,
    )


def per_device(
    residual,
    queries,
    kv_cache,
    kv_pages,
    cache_len,
    page_row,
    page_len,
    routes,
    route_weight,
    out_weight,
    gate_weight,
    up_weight,
    down_weight,
):
    pool_size = lax.axis_size("pool")
    expert_size = lax.axis_size("expert")
    pool_index = lax.axis_index("pool")
    expert_index = lax.axis_index("expert")
    cores, near = 2, 2
    outer, far = pool_size // cores, expert_size // near
    core = pool_index % cores

    def swap(value, pool_flip=0, expert_flip=0):
        pairs = []
        for p in range(pool_size):
            for e in range(expert_size):
                pairs.append((p * expert_size + e, (p ^ pool_flip) * expert_size + (e ^ expert_flip)))
        return lax.ppermute(value, ("pool", "expert"), pairs)

    rows, steps, heads, head_dim = queries.shape
    length, kv_heads = kv_cache.shape[1:3]
    held, _, page_size = kv_pages.shape[:3]
    width = residual.shape[2]
    half = width // cores
    tokens = rows * steps
    scale = 1.0 / math.sqrt(head_dim)

    def head_of(pool):
        return pool * kv_heads // pool_size

    def pages_for(pool):
        picked = lax.dynamic_index_in_dim(kv_pages[:, 0], head_of(pool), 2, keepdims=False)
        return picked.reshape(held * page_size * 2, head_dim)

    my_head = head_of(pool_index)
    experts = gate_weight.shape[0] * expert_size
    first = (pool_index // cores == 0).astype(jnp.int32)
    whence = [pool_index ^ (k * cores) for k in range(outer)]
    whence += [p ^ 1 for p in whence]
    info = jnp.stack([core, first, expert_index, jnp.int32(experts), my_head] + whence)
    own_pages = pages_for(pool_index)
    sets = [own_pages]
    for k in range(1, outer):
        flip = k * cores
        sets.append(swap(pages_for(pool_index ^ flip), flip))
    for n in range(outer):
        sets.append(swap(sets[n], 1))

    group = steps * heads
    everything = rows * group
    q_rows = queries.reshape(everything, head_dim)
    deep = length * kv_heads * 2
    kv_rows = kv_cache.reshape(rows, deep, head_dim)
    stat = jax.ShapeDtypeStruct((everything, head_dim), float32)
    lens, owners, sizes = far_off(cache_len), far_off(page_row[:, 0]), far_off(page_len[:, 0])
    weight_half = jax.ShapeDtypeStruct((out_weight.shape[0], half), bfloat16)
    acc, top, total, weight_send, weight_keep, own_residual = call(
        functools.partial(cache_kernel, heads, kv_heads, pool_size, scale),
        (stat, stat, stat, weight_half, weight_half, jax.ShapeDtypeStruct((tokens, half), bfloat16)),
        [SMEM] * 4 + [HBM, VMEM, HBM, HBM, HBM],
        scratch=[
            pltpu.VMEM(kv_rows.shape, bfloat16),
            pltpu.VMEM(q_rows.shape, bfloat16),
            pltpu.SemaphoreType.DMA((rows,)),
            pltpu.SemaphoreType.DMA((2, 4)),
            pltpu.SemaphoreType.DMA((2,)),
        ],
        vmem=24,
        flops=4 * everything * deep * head_dim,
        bytes_accessed=kv_cache.size * 2 + out_weight.size * 2,
    )(info, lens, owners, sizes, far_off(q_rows), own_pages, far_off(kv_rows), far_off(out_weight), far_off(residual.reshape(tokens, width)))
    low, send = call(
        functools.partial(page_kernel, heads, group, pool_size, scale),
        (
            jax.ShapeDtypeStruct((tokens, heads * head_dim), bfloat16),
            jax.ShapeDtypeStruct((tokens, half), bfloat16),
        ),
        [SMEM] * 3 + [VMEM] * (4 + pool_size),
        scratch=[pltpu.VMEM((everything, head_dim), float32)] * 3,
        flops=2 * tokens * heads * head_dim * half,
    )(info, owners, sizes, q_rows, acc, top, total, *sets[1:], weight_send)
    arrived = swap(send, 1)
    keep = call(
        project_kernel, jax.ShapeDtypeStruct((tokens, half), float32), [SMEM, VMEM, VMEM, VMEM],
        flops=2 * tokens * heads * head_dim * half,
    )(info, low, weight_keep, own_residual)

    wide = -(-2 * experts // LANES) * LANES
    routes = routes.reshape(tokens, -1)
    named = routes[:, :, None] == jnp.arange(wide, dtype=jnp.int32) % experts
    table = jnp.sum(jnp.where(named, route_weight.reshape(tokens, -1, 1), 0.0), axis=1)
    coarse = lax.reduce_precision(table, 8, 7)
    table = jnp.where(jnp.arange(wide) < experts, coarse, jnp.where(jnp.arange(wide) < 2 * experts, table - coarse, 0.0))

    partial = keep + arrived.astype(float32)
    message = jnp.concatenate([partial, table], axis=1).astype(bfloat16)

    got = {(0, 0): message}
    for e in range(near):
        for k in range(outer):
            if k or e:
                got[k, e] = swap(message, k * cores, e)
    hiddens = []
    for e in range(near):
        total = got[0, e][:, :half].astype(float32)
        for k in range(1, outer):
            total = total + got[k, e][:, :half].astype(float32)
        hiddens.append(total)
    block_low = jnp.concatenate(
        [jnp.concatenate([hiddens[e].astype(bfloat16), got[0, e][:, half:]], axis=1) for e in range(near)], axis=0
    )
    gate_near, up_near, down_near = call(
        functools.partial(load_kernel, 3),
        tuple(jax.ShapeDtypeStruct(w.shape, bfloat16) for w in (gate_weight, up_weight, down_weight)),
        [ANY] + [HBM] * 3,
        scratch=[pltpu.SemaphoreType.DMA((3, 4, gate_weight.shape[0]))],
        vmem=16,
        bytes_accessed=6 * gate_weight.size,
    )(block_low, far_off(gate_weight), far_off(up_weight), far_off(down_weight))
    blocks = [block_low] + [swap(block_low, 0, k * near) for k in range(1, far)]
    others = [swap(b, 1) for b in blocks]

    everyone = tokens * near * far
    units = gate_weight.shape[0] * gate_weight.shape[2]
    act, outgoing = call(
        functools.partial(expert_kernel, far),
        (
            jax.ShapeDtypeStruct((everyone, units), bfloat16),
            jax.ShapeDtypeStruct((everyone, half), bfloat16),
        ),
        [SMEM] + [VMEM] * (2 * far + 3),
        vmem=24,
        flops=4 * everyone * width * units,
    )(info, *blocks, *others, gate_near, up_near, down_near)
    incoming = swap(outgoing, 1)
    kept = call(
        down_kernel, jax.ShapeDtypeStruct((everyone, half), bfloat16), [SMEM, VMEM, VMEM], vmem=16,
        flops=2 * everyone * half * units,
    )(info, act, down_near)
    summed = (kept.astype(float32) + incoming.astype(float32)).reshape(far, near * tokens, half)
    back = summed[0]
    for k in range(1, far):
        back = back + swap(summed[k].astype(bfloat16), 0, k * near).astype(float32)
    back = back.reshape(near, tokens, half)
    result = back[0] + hiddens[0]
    for e in range(near):
        for k in range(outer):
            if k or e:
                result = result + swap(back[e].astype(bfloat16), k * cores, e).astype(float32)
    mine = result.astype(bfloat16)
    theirs = swap(mine, 1)
    output = jnp.where(
        core == 0, jnp.concatenate([mine, theirs], axis=1), jnp.concatenate([theirs, mine], axis=1)
    )
    return output.reshape(rows, steps, width)


def solution(mesh):
    return jax.shard_map(
        per_device,
        mesh=mesh,
        in_specs=(
            P("expert", None, None),
            P("expert", None, "pool", None),
            P("expert", None, None, None, None),
            P("pool", "expert", None, None, None, None),
            P("expert"),
            P(None, "expert"),
            P(None, "expert"),
            P("expert", None, None),
            P("expert", None, None),
            P("pool", None),
            P("expert", None, "pool"),
            P("expert", None, "pool"),
            P("expert", "pool", None),
        ),
        out_specs=P("expert", None, None),
        check_vma=False,
    )
```

```python
import functools
import math

import jax
import jax.numpy as jnp
from jax import lax
from jax.experimental import pallas as pl
from jax.experimental.pallas import tpu as pltpu
from jax.sharding import PartitionSpec as P

MIB = 1 << 20
LANES = 128
very_low = -1e30
cores = 2
near = 2
VMEM = pl.BlockSpec(memory_space=pltpu.VMEM)
HBM = pl.BlockSpec(memory_space=pltpu.HBM)
ANY = pl.BlockSpec(memory_space=pl.ANY)
float32 = jnp.float32
bfloat16 = jnp.bfloat16


def far_off(array):
    return pltpu.with_memory_space_constraint(array, pltpu.HBM)


def dot_t(a, b):
    return lax.dot_general(a, b, (((1,), (1,)), ((), ())), preferred_element_type=float32)


def dot(a, b):
    return jnp.dot(a, b, preferred_element_type=float32)


def slice_kernel(kv_heads, pages_hbm, own_ref, *rest):
    others, sem = rest[:-1], rest[-1]
    pool_size = lax.axis_size("pool")
    me = lax.axis_index("pool")
    copies = []
    for k, dest in enumerate((own_ref,) + others):
        head = (me ^ (k * cores)) * kv_heads // pool_size
        copies.append(pltpu.make_async_copy(pages_hbm.at[:, 0, :, head], dest, sem.at[k]))
    for copy in copies[::-1]:
        copy.start()
    for copy in copies:
        copy.wait()


def cache_kernel(
    scale, len_hbm, row_hbm, size_hbm, q_hbm, own_ref, kv_hbm, weight_hbm, residual_hbm,
    acc_ref, top_ref, total_ref, q_ref, owner_ref, send_ref, keep_ref, residual_ref,
    kv_ref, raw_ref, score_ref, low_ref, len_ref, row_ref, size_ref, small_sem, kv_sem, weight_sem,
):
    rows, length, kv_heads = kv_hbm.shape[:3]
    head_dim = kv_hbm.shape[4]
    pool_size = lax.axis_size("pool")
    me = lax.axis_index("pool")
    core = me % cores
    head = me * kv_heads // pool_size
    small = [
        pltpu.make_async_copy(len_hbm, len_ref, small_sem.at[0]),
        pltpu.make_async_copy(row_hbm, row_ref, small_sem.at[1]),
        pltpu.make_async_copy(size_hbm, size_ref, small_sem.at[2]),
        pltpu.make_async_copy(q_hbm, q_ref, small_sem.at[3]),
    ]
    for copy in small:
        copy.start()
    copies = [pltpu.make_async_copy(kv_hbm.at[r, :, head], kv_ref.at[r], kv_sem.at[r]) for r in range(rows)]
    for copy in copies:
        copy.start()
    chunks = weight_sem.shape[1]
    deep = weight_hbm.shape[0] // chunks
    half = send_ref.shape[1]
    mine = pl.ds(pl.multiple_of(core * half, half), half)
    theirs = pl.ds(pl.multiple_of((1 - core) * half, half), half)
    weights_in = [pltpu.make_async_copy(residual_hbm.at[:, :, mine], raw_ref, small_sem.at[4])]
    for side, (columns, target) in enumerate(((theirs, send_ref), (mine, keep_ref))):
        for n in range(chunks):
            part = pl.ds(n * deep, deep)
            weights_in.append(
                pltpu.make_async_copy(weight_hbm.at[part, columns], target.at[part], weight_sem.at[side, n])
            )
    for copy in weights_in:
        copy.start()
    for copy in small:
        copy.wait()
    everything = q_ref.shape[0]
    group = everything // rows
    steps = residual_hbm.shape[1]
    deep = 2 * length
    kv_rows = kv_ref.reshape(rows, deep, head_dim)
    page_rows = own_ref.shape[0]
    held = row_ref.shape[0] // pool_size
    span = page_rows // held
    page_lane = lax.broadcasted_iota(jnp.int32, (8, span), 1)
    page_key = jnp.where(page_lane % 2 == 0, page_lane // 2, span)
    owners = []
    for k in range(pool_size):
        source = me ^ (k * cores if k * cores < pool_size else (k * cores) % pool_size + 1)
        for i in range(held):
            page = source * held + i
            owners.append(jnp.where(page_key < size_ref[page], row_ref[page], -1))
    owner_ref[...] = jnp.concatenate(owners[held:], axis=1)
    own_owner = jnp.concatenate(owners[:held], axis=1)[:1]
    lane = lax.broadcasted_iota(jnp.int32, (1, deep), 1)
    key = jnp.where(lane % 2 == 0, lane // 2, 2 * length)
    step = lax.broadcasted_iota(jnp.int32, (group, 1), 0) // (group // steps)
    score_ref[:, deep:] = dot_t(q_ref[...], own_ref[...])
    here = [slice(r * group, (r + 1) * group) for r in range(rows)]
    for r in range(rows):
        copies[r].wait()
        score_ref[here[r], :deep] = dot_t(q_ref[here[r], :], kv_rows[r])
    for r in range(rows):
        scores = score_ref[here[r], :] * scale
        seen = jnp.concatenate(
            [key <= len_ref[r] + step, jnp.broadcast_to(own_owner == r, (group, page_rows))], axis=1
        )
        scores = jnp.where(seen, scores, very_low)
        top = jnp.max(scores, axis=1, keepdims=True)
        weights = jnp.where(seen, jnp.exp(scores - top), 0.0)
        total = jnp.sum(weights, axis=1, keepdims=True)
        low_ref[here[r], :] = pltpu.roll(weights, 1, 1).astype(bfloat16)
        top_ref[here[r], :] = jnp.broadcast_to(top, (group, top_ref.shape[1]))
        total_ref[here[r], :] = jnp.broadcast_to(total, (group, total_ref.shape[1]))
    acc_ref[...] = dot(low_ref[:, deep:], own_ref[...])
    for r in range(rows):
        acc_ref[here[r], :] += dot(low_ref[here[r], :deep], kv_rows[r])
    for copy in weights_in:
        copy.wait()
    first = jnp.where(me // cores == 0, 1.0, 0.0)
    residual_ref[...] = raw_ref.reshape(*residual_ref.shape)[...].astype(float32) * first


def page_kernel(heads, rows, scale, q_ref, acc_in, top_in, total_in, owner_ref, *rest):
    pages = rest[:-6]
    weight_ref, low_ref, send_ref, score_ref, chance_ref, flat_ref = rest[-6:]
    everything, head_dim = q_ref.shape
    group = everything // rows
    size = pages[0].shape[0]
    for n, page in enumerate(pages):
        score_ref[:, n * size : (n + 1) * size] = dot_t(q_ref[...], page[...])
    owner = owner_ref[:1, :]
    for r in range(rows):
        here = slice(r * group, (r + 1) * group)
        seen = jnp.broadcast_to(owner == r, (group, owner.shape[1]))
        scores = jnp.where(seen, score_ref[here, :] * scale, very_low)
        top = jnp.maximum(top_in[here, :], jnp.max(scores, axis=1, keepdims=True))
        weights = jnp.where(seen, jnp.exp(scores - top[:, :1]), 0.0)
        shrink = jnp.exp(top_in[here, :] - top)
        total = total_in[here, :] * shrink + jnp.sum(weights, axis=1, keepdims=True)
        chance_ref[here, :] = pltpu.roll(weights, 1, 1).astype(bfloat16)
        inverse = 1.0 / total
        flat_ref[0, here, :] = inverse
        flat_ref[1, here, :] = acc_in[here, :] * shrink * inverse
    mixed = dot(chance_ref[:, :size], pages[0][...])
    for n in range(1, len(pages)):
        mixed = mixed + dot(chance_ref[:, n * size : (n + 1) * size], pages[n][...])
    flat_ref[1] = flat_ref[1] + mixed * flat_ref[0]
    tokens = everything // heads
    low = jnp.concatenate(
        [flat_ref[1, pl.ds(h, tokens, stride=heads), :].astype(bfloat16) for h in range(heads)], axis=1
    )
    low_ref[...] = low
    send_ref[...] = dot(low, weight_ref[...]).astype(bfloat16)


def load_kernel(count, *refs):
    sources, dests, sems = refs[1 : 1 + count], refs[1 + count : 1 + 2 * count], refs[-1]
    chunks = sems.shape[1]
    copies = []
    for n in range(count):
        for j in range(sources[n].shape[0]):
            size = sources[n].shape[1] // chunks
            for i in range(chunks):
                part = pl.ds(i * size, size)
                copies.append(
                    pltpu.make_async_copy(sources[n].at[j, part], dests[n].at[j, part], sems.at[n, i, j])
                )
    for copy in copies:
        copy.start()
    for copy in copies:
        copy.wait()


def project_kernel(low_ref, weight_ref, residual_ref, keep_ref):
    keep_ref[...] = dot(low_ref[...], weight_ref[...]) + residual_ref[...]


def expert_kernel(own_ref, other_ref, gate_ref, up_ref, down_ref, act_ref, send_ref):
    half = send_ref.shape[1]
    own = own_ref[:, :half]
    other = other_ref[:, :half]
    table = own_ref[:, half:].astype(float32)
    lane = lax.broadcasted_iota(jnp.int32, table.shape, 1)
    core = lax.axis_index("pool") % cores
    first = pl.ds(pl.multiple_of(core * half, half), half)
    second = pl.ds(pl.multiple_of((1 - core) * half, half), half)
    experts, _, units = gate_ref.shape
    everyone = experts * lax.axis_size("expert")
    for j in range(experts):
        mine = lax.axis_index("expert") * experts + j
        weight = jnp.sum(
            jnp.where((lane == mine) | (lane == mine + everyone), table, 0.0), axis=1, keepdims=True
        )
        gate = dot(own, gate_ref[j, first, :]) + dot(other, gate_ref[j, second, :])
        up = dot(own, up_ref[j, first, :]) + dot(other, up_ref[j, second, :])
        active = gate / (1.0 + jnp.exp(-gate)) * up
        act_ref[:, j * units : (j + 1) * units] = (active * weight).astype(bfloat16)
    total = 0.0
    for j in range(experts):
        total = total + dot(act_ref[:, j * units : (j + 1) * units], down_ref[j, :, second])
    send_ref[...] = total.astype(bfloat16)


def down_kernel(act_ref, down_ref, keep_ref):
    half = keep_ref.shape[1]
    experts, units, _ = down_ref.shape
    core = lax.axis_index("pool") % cores
    first = pl.ds(pl.multiple_of(core * half, half), half)
    total = 0.0
    for j in range(experts):
        total = total + dot(act_ref[:, j * units : (j + 1) * units], down_ref[j, :, first])
    keep_ref[...] = total


def finish_kernel(mine_ref, theirs_ref, out_ref):
    tokens, half = mine_ref.shape
    core = lax.axis_index("pool") % cores
    flat = out_ref.reshape(tokens, out_ref.shape[2])
    flat[:, pl.ds(pl.multiple_of(core * half, half), half)] = mine_ref[...]
    flat[:, pl.ds(pl.multiple_of((1 - core) * half, half), half)] = theirs_ref[...]


def call(kernel, outs, specs, scratch=(), vmem=16, flops=0, bytes_accessed=0, **kw):
    return pl.pallas_call(
        kernel,
        out_shape=outs,
        in_specs=specs,
        out_specs=jax.tree.map(lambda _: VMEM, outs),
        scratch_shapes=scratch,
        compiler_params=pltpu.CompilerParams(vmem_limit_bytes=vmem * MIB),
        cost_estimate=pl.CostEstimate(flops=flops, bytes_accessed=bytes_accessed, transcendentals=0),
        **kw,
    )


def per_device(
    residual,
    queries,
    kv_cache,
    kv_pages,
    cache_len,
    page_row,
    page_len,
    routes,
    route_weight,
    out_weight,
    gate_weight,
    up_weight,
    down_weight,
):
    pool_size = lax.axis_size("pool")
    expert_size = lax.axis_size("expert")
    outer, far = pool_size // cores, expert_size // near

    def swap(value, pool_flip=0, expert_flip=0):
        pairs = []
        for p in range(pool_size):
            for e in range(expert_size):
                pairs.append((p * expert_size + e, (p ^ pool_flip) * expert_size + (e ^ expert_flip)))
        return lax.ppermute(value, ("pool", "expert"), pairs)

    rows, steps, heads, head_dim = queries.shape
    length, kv_heads = kv_cache.shape[1:3]
    held, _, page_size = kv_pages.shape[:3]
    width = residual.shape[2]
    half = width // cores
    tokens = rows * steps
    scale = 1.0 / math.sqrt(head_dim)

    page_rows = held * page_size * 2
    piece = jax.ShapeDtypeStruct((held, page_size, 2, head_dim), bfloat16)
    sliced = call(
        functools.partial(slice_kernel, kv_heads),
        (piece,) * outer,
        [HBM],
        scratch=[pltpu.SemaphoreType.DMA((outer,))],
        vmem=4,
        bytes_accessed=2 * kv_pages.size,
    )(far_off(kv_pages))
    sliced = [p.reshape(page_rows, head_dim) for p in sliced]
    sets = [sliced[0]]
    for k in range(1, outer):
        with jax.named_scope("pages"):
            sets.append(swap(sliced[k], k * cores))
    for k in range(outer):
        with jax.named_scope("pages"):
            sets.append(swap(sliced[k], k * cores + 1))

    group = steps * heads
    everything = rows * group
    stat = jax.ShapeDtypeStruct((everything, head_dim), float32)
    weight_half = jax.ShapeDtypeStruct((out_weight.shape[0], half), bfloat16)
    q_shape = jax.ShapeDtypeStruct((everything, head_dim), bfloat16)
    other_lanes = (pool_size - 1) * page_rows
    lanes = 2 * length + page_rows
    acc, top, total, q, owner, weight_send, weight_keep, own_residual = call(
        functools.partial(cache_kernel, scale),
        (
            stat, stat, stat, q_shape, jax.ShapeDtypeStruct((8, other_lanes), jnp.int32), weight_half, weight_half,
            jax.ShapeDtypeStruct((tokens, half), float32),
        ),
        [HBM] * 4 + [VMEM] + [HBM] * 3,
        scratch=[
            pltpu.VMEM((rows, length, 2, head_dim), bfloat16),
            pltpu.VMEM((rows, steps, half), bfloat16),
            pltpu.VMEM((everything, lanes), float32),
            pltpu.VMEM((everything, lanes), bfloat16),
            pltpu.SMEM((rows,), jnp.int32),
            pltpu.SMEM(page_row[:, 0].shape, jnp.int32),
            pltpu.SMEM(page_len[:, 0].shape, jnp.int32),
            pltpu.SemaphoreType.DMA((5,)),
            pltpu.SemaphoreType.DMA((rows,)),
            pltpu.SemaphoreType.DMA((2, 4)),
        ],
        vmem=24,
        flops=4 * everything * lanes * head_dim,
        bytes_accessed=kv_cache.size + out_weight.size * 2,
    )(
        far_off(cache_len), far_off(page_row[:, 0]), far_off(page_len[:, 0]),
        far_off(queries.reshape(everything, head_dim)), sets[0], far_off(kv_cache), far_off(out_weight),
        far_off(residual),
    )
    low, send = call(
        functools.partial(page_kernel, heads, rows, scale),
        (
            jax.ShapeDtypeStruct((tokens, heads * head_dim), bfloat16),
            jax.ShapeDtypeStruct((tokens, half), bfloat16),
        ),
        [VMEM] * (5 + pool_size),
        scratch=[
            pltpu.VMEM((everything, other_lanes), float32),
            pltpu.VMEM((everything, other_lanes), bfloat16),
            pltpu.VMEM((2, everything, head_dim), float32),
        ],
        flops=2 * tokens * heads * head_dim * half,
    )(q, acc, top, total, owner, *sets[1:], weight_send)
    arrived = swap(send, 1)
    keep = call(
        project_kernel, jax.ShapeDtypeStruct((tokens, half), float32), [VMEM] * 3,
        flops=2 * tokens * heads * head_dim * half,
    )(low, weight_keep, own_residual)

    experts = gate_weight.shape[0] * expert_size
    wide = -(-2 * experts // LANES) * LANES
    routes = routes.reshape(tokens, -1)
    named = routes[:, :, None] == jnp.arange(wide, dtype=jnp.int32) % experts
    table = jnp.sum(jnp.where(named, route_weight.reshape(tokens, -1, 1), 0.0), axis=1)
    coarse = lax.reduce_precision(table, 8, 7)
    table = jnp.where(jnp.arange(wide) < experts, coarse, jnp.where(jnp.arange(wide) < 2 * experts, table - coarse, 0.0))

    partial = keep + arrived.astype(float32)
    summed = partial.astype(bfloat16)
    hidden = summed.astype(float32)
    for k in range(1, outer):
        hidden = hidden + swap(summed, k * cores).astype(float32)
    message = jnp.concatenate([hidden, table], axis=1).astype(bfloat16)
    gate_near, up_near, down_near = gate_weight, up_weight, down_weight
    flips = list(range(expert_size - 1, 0, -1))
    blocks = {0: message}
    for k in flips:
        with jax.named_scope("far" if k >= expert_size // 2 else "close"):
            blocks[k] = swap(message, 0, k)
    units = gate_weight.shape[0] * gate_weight.shape[2]
    count = expert_size // 2
    result = 0.0
    early = flips[: count - 1] + [0]
    for batch in (early, flips[count - 1 :]):
        own = jnp.concatenate([blocks[k] for k in batch], axis=0)
        other = swap(own, 1)
        here = count * tokens
        act, outgoing = call(
            expert_kernel,
            (jax.ShapeDtypeStruct((here, units), bfloat16), jax.ShapeDtypeStruct((here, half), bfloat16)),
            [VMEM] * 5,
            flops=5 * here * width * units,
        )(own, other, gate_near, up_near, down_near)
        incoming = swap(outgoing, 1)
        kept = call(
            down_kernel, jax.ShapeDtypeStruct((here, half), float32), [VMEM] * 2, flops=2 * here * half * units
        )(act, down_near)
        total = kept + incoming.astype(float32)
        for n, k in enumerate(batch):
            part = total[n * tokens : (n + 1) * tokens]
            if k:
                with jax.named_scope("home"):
                    part = swap(part.astype(bfloat16), 0, k).astype(float32)
            result = result + part
    outcome = result.astype(bfloat16)
    result = hidden + result
    for k in range(1, outer):
        result = result + swap(outcome, k * cores).astype(float32)
    mine = result.astype(bfloat16)
    theirs = swap(mine, 1)
    return call(
        finish_kernel, jax.ShapeDtypeStruct(residual.shape, bfloat16), [VMEM] * 2, vmem=4, bytes_accessed=4 * residual.size
    )(mine, theirs)


def solution(mesh):
    return jax.shard_map(
        per_device,
        mesh=mesh,
        in_specs=(
            P("expert", None, None),
            P("expert", None, "pool", None),
            P("expert", None, None, None, None),
            P("pool", "expert", None, None, None, None),
            P("expert"),
            P(None, "expert"),
            P(None, "expert"),
            P("expert", None, None),
            P("expert", None, None),
            P("pool", None),
            P("expert", None, "pool"),
            P("expert", None, "pool"),
            P("expert", "pool", None),
        ),
        out_specs=P("expert", None, None),
        check_vma=False,
    )
```

```python
import functools
import math

import jax
import jax.numpy as jnp
from jax import lax
from jax.experimental import pallas as pl
from jax.experimental.pallas import tpu as pltpu
from jax.sharding import PartitionSpec as P


MIB = 1 << 20
LANES = 128
very_low = -1e30
cores = 2
near = 2
VMEM = pl.BlockSpec(memory_space=pltpu.VMEM)
HBM = pl.BlockSpec(memory_space=pltpu.HBM)
ANY = pl.BlockSpec(memory_space=pl.ANY)
float32 = jnp.float32
bfloat16 = jnp.bfloat16


def far_off(array):
    return pltpu.with_memory_space_constraint(array, pltpu.HBM)


def dot_t(a, b):
    return lax.dot_general(a, b, (((1,), (1,)), ((), ())), preferred_element_type=float32)


def dot(a, b):
    return jnp.dot(a, b, preferred_element_type=float32)


def slice_kernel(kv_heads, pages_hbm, own_ref, *rest):
    others, sem = rest[:-1], rest[-1]
    pool_size = lax.axis_size("pool")
    me = lax.axis_index("pool")
    copies = []
    for k, dest in enumerate((own_ref,) + others):
        head = (me ^ (k * cores)) * kv_heads // pool_size
        copies.append(pltpu.make_async_copy(pages_hbm.at[:, 0, :, head], dest, sem.at[k]))
    for copy in copies[::-1]:
        copy.start()
    for copy in copies:
        copy.wait()


def cache_kernel(
    scale, len_hbm, row_hbm, size_hbm, q_hbm, own_ref, kv_hbm, weight_hbm, residual_hbm,
    acc_ref, top_ref, total_ref, q_ref, owner_ref, send_ref, keep_ref, residual_ref,
    kv_ref, raw_ref, score_ref, low_ref, len_ref, row_ref, size_ref, small_sem, kv_sem, weight_sem,
):
    rows, length, kv_heads = kv_hbm.shape[:3]
    head_dim = kv_hbm.shape[4]
    pool_size = lax.axis_size("pool")
    me = lax.axis_index("pool")
    core = me % cores
    head = me * kv_heads // pool_size
    small = [
        pltpu.make_async_copy(len_hbm, len_ref, small_sem.at[0]),
        pltpu.make_async_copy(row_hbm, row_ref, small_sem.at[1]),
        pltpu.make_async_copy(size_hbm, size_ref, small_sem.at[2]),
        pltpu.make_async_copy(q_hbm, q_ref, small_sem.at[3]),
    ]
    for copy in small:
        copy.start()
    copies = [pltpu.make_async_copy(kv_hbm.at[r, :, head], kv_ref.at[r], kv_sem.at[r]) for r in range(rows)]
    for copy in copies:
        copy.start()
    chunks = weight_sem.shape[1]
    deep = weight_hbm.shape[0] // chunks
    half = send_ref.shape[1]
    mine = pl.ds(pl.multiple_of(core * half, half), half)
    theirs = pl.ds(pl.multiple_of((1 - core) * half, half), half)
    weights_in = [pltpu.make_async_copy(residual_hbm.at[:, :, mine], raw_ref, small_sem.at[4])]
    for side, (columns, target) in enumerate(((theirs, send_ref), (mine, keep_ref))):
        for n in range(chunks):
            part = pl.ds(n * deep, deep)
            weights_in.append(
                pltpu.make_async_copy(weight_hbm.at[part, columns], target.at[part], weight_sem.at[side, n])
            )
    for copy in weights_in:
        copy.start()
    for copy in small:
        copy.wait()
    everything = q_ref.shape[0]
    group = everything // rows
    steps = residual_hbm.shape[1]
    deep = 2 * length
    kv_rows = kv_ref.reshape(rows, deep, head_dim)
    page_rows = own_ref.shape[0]
    held = row_ref.shape[0] // pool_size
    span = page_rows // held
    page_lane = lax.broadcasted_iota(jnp.int32, (8, span), 1)
    page_key = jnp.where(page_lane % 2 == 0, page_lane // 2, span)
    owners = []
    for k in range(pool_size):
        source = me ^ (k * cores if k * cores < pool_size else (k * cores) % pool_size + 1)
        for i in range(held):
            page = source * held + i
            owners.append(jnp.where(page_key < size_ref[page], row_ref[page], -1))
    owner_ref[...] = jnp.concatenate(owners[held:], axis=1)
    own_owner = jnp.concatenate(owners[:held], axis=1)[:1]
    lane = lax.broadcasted_iota(jnp.int32, (1, deep), 1)
    key = jnp.where(lane % 2 == 0, lane // 2, 2 * length)
    step = lax.broadcasted_iota(jnp.int32, (group, 1), 0) // (group // steps)
    score_ref[:, deep:] = dot_t(q_ref[...], own_ref[...])
    here = [slice(r * group, (r + 1) * group) for r in range(rows)]
    for r in range(rows):
        copies[r].wait()
        score_ref[here[r], :deep] = dot_t(q_ref[here[r], :], kv_rows[r])
    for r in range(rows):
        scores = score_ref[here[r], :] * scale
        seen = jnp.concatenate(
            [key <= len_ref[r] + step, jnp.broadcast_to(own_owner == r, (group, page_rows))], axis=1
        )
        scores = jnp.where(seen, scores, very_low)
        top = jnp.max(scores, axis=1, keepdims=True)
        weights = jnp.where(seen, jnp.exp(scores - top), 0.0)
        total = jnp.sum(weights, axis=1, keepdims=True)
        low_ref[here[r], :] = pltpu.roll(weights, 1, 1).astype(bfloat16)
        top_ref[here[r], :] = jnp.broadcast_to(top, (group, top_ref.shape[1]))
        total_ref[here[r], :] = jnp.broadcast_to(total, (group, total_ref.shape[1]))
    acc_ref[...] = dot(low_ref[:, deep:], own_ref[...])
    for r in range(rows):
        acc_ref[here[r], :] += dot(low_ref[here[r], :deep], kv_rows[r])
    for copy in weights_in:
        copy.wait()
    first = jnp.where(me // cores == 0, 1.0, 0.0)
    residual_ref[...] = raw_ref.reshape(*residual_ref.shape)[...].astype(float32) * first


def page_kernel(heads, rows, scale, q_ref, acc_in, top_in, total_in, owner_ref, *rest):
    pages = rest[:-6]
    weight_ref, low_ref, send_ref, score_ref, chance_ref, flat_ref = rest[-6:]
    everything, _ = q_ref.shape
    group = everything // rows
    size = pages[0].shape[0]
    for n, page in enumerate(pages):
        score_ref[:, n * size : (n + 1) * size] = dot_t(q_ref[...], page[...])
    owner = owner_ref[:1, :]
    for r in range(rows):
        here = slice(r * group, (r + 1) * group)
        seen = jnp.broadcast_to(owner == r, (group, owner.shape[1]))
        scores = jnp.where(seen, score_ref[here, :] * scale, very_low)
        top = jnp.maximum(top_in[here, :], jnp.max(scores, axis=1, keepdims=True))
        weights = jnp.where(seen, jnp.exp(scores - top[:, :1]), 0.0)
        shrink = jnp.exp(top_in[here, :] - top)
        total = total_in[here, :] * shrink + jnp.sum(weights, axis=1, keepdims=True)
        chance_ref[here, :] = pltpu.roll(weights, 1, 1).astype(bfloat16)
        inverse = 1.0 / total
        flat_ref[0, here, :] = inverse
        flat_ref[1, here, :] = acc_in[here, :] * shrink * inverse
    mixed = dot(chance_ref[:, :size], pages[0][...])
    for n in range(1, len(pages)):
        mixed = mixed + dot(chance_ref[:, n * size : (n + 1) * size], pages[n][...])
    flat_ref[1] = flat_ref[1] + mixed * flat_ref[0]
    tokens = everything // heads
    low = jnp.concatenate(
        [flat_ref[1, pl.ds(h, tokens, stride=heads), :].astype(bfloat16) for h in range(heads)], axis=1
    )
    low_ref[...] = low
    send_ref[...] = dot(low, weight_ref[...]).astype(bfloat16)


def project_kernel(low_ref, weight_ref, residual_ref, keep_ref):
    keep_ref[...] = dot(low_ref[...], weight_ref[...]) + residual_ref[...]


def expert_kernel(own_ref, other_ref, gate_ref, up_ref, down_ref, act_ref, send_ref):
    half = send_ref.shape[1]
    own = own_ref[:, :half]
    other = other_ref[:, :half]
    table = own_ref[:, half:].astype(float32)
    lane = lax.broadcasted_iota(jnp.int32, table.shape, 1)
    core = lax.axis_index("pool") % cores
    first = pl.ds(pl.multiple_of(core * half, half), half)
    second = pl.ds(pl.multiple_of((1 - core) * half, half), half)
    experts, _, units = gate_ref.shape
    everyone = experts * lax.axis_size("expert")
    for j in range(experts):
        mine = lax.axis_index("expert") * experts + j
        weight = jnp.sum(
            jnp.where((lane == mine) | (lane == mine + everyone), table, 0.0), axis=1, keepdims=True
        )
        gate = dot(own, gate_ref[j, first, :]) + dot(other, gate_ref[j, second, :])
        up = dot(own, up_ref[j, first, :]) + dot(other, up_ref[j, second, :])
        active = gate / (1.0 + jnp.exp(-gate)) * up
        act_ref[:, j * units : (j + 1) * units] = (active * weight).astype(bfloat16)
    total = 0.0
    for j in range(experts):
        total = total + dot(act_ref[:, j * units : (j + 1) * units], down_ref[j, :, second])
    send_ref[...] = total.astype(bfloat16)


def down_kernel(act_ref, down_ref, keep_ref):
    half = keep_ref.shape[1]
    experts, units, _ = down_ref.shape
    core = lax.axis_index("pool") % cores
    first = pl.ds(pl.multiple_of(core * half, half), half)
    total = 0.0
    for j in range(experts):
        total = total + dot(act_ref[:, j * units : (j + 1) * units], down_ref[j, :, first])
    keep_ref[...] = total


def finish_kernel(mine_ref, theirs_ref, out_ref):
    tokens, half = mine_ref.shape
    core = lax.axis_index("pool") % cores
    flat = out_ref.reshape(tokens, out_ref.shape[2])
    flat[:, pl.ds(pl.multiple_of(core * half, half), half)] = mine_ref[...]
    flat[:, pl.ds(pl.multiple_of((1 - core) * half, half), half)] = theirs_ref[...]


def call(kernel, outs, specs, scratch=(), vmem=16, flops=0, bytes_accessed=0, **kw):
    return pl.pallas_call(
        kernel,
        out_shape=outs,
        in_specs=specs,
        out_specs=jax.tree.map(lambda _: VMEM, outs),
        scratch_shapes=scratch,
        compiler_params=pltpu.CompilerParams(vmem_limit_bytes=vmem * MIB),
        cost_estimate=pl.CostEstimate(flops=flops, bytes_accessed=bytes_accessed, transcendentals=0),
        **kw,
    )


def per_device(
    residual,
    queries,
    kv_cache,
    kv_pages,
    cache_len,
    page_row,
    page_len,
    routes,
    route_weight,
    out_weight,
    gate_weight,
    up_weight,
    down_weight,
):
    pool_size = lax.axis_size("pool")
    expert_size = lax.axis_size("expert")
    outer, far = pool_size // cores, expert_size // near

    def swap(value, pool_flip=0, expert_flip=0):
        pairs = []
        for p in range(pool_size):
            for e in range(expert_size):
                pairs.append((p * expert_size + e, (p ^ pool_flip) * expert_size + (e ^ expert_flip)))
        return lax.ppermute(value, ("pool", "expert"), pairs)

    rows, steps, heads, head_dim = queries.shape
    length, kv_heads = kv_cache.shape[1:3]
    held, _, page_size = kv_pages.shape[:3]
    width = residual.shape[2]
    half = width // cores
    tokens = rows * steps
    scale = 1.0 / math.sqrt(head_dim)

    page_rows = held * page_size * 2
    piece = jax.ShapeDtypeStruct((held, page_size, 2, head_dim), bfloat16)
    sliced = call(
        functools.partial(slice_kernel, kv_heads),
        (piece,) * outer,
        [HBM],
        scratch=[pltpu.SemaphoreType.DMA((outer,))],
        vmem=4,
        bytes_accessed=2 * kv_pages.size,
    )(far_off(kv_pages))
    sliced = [p.reshape(page_rows, head_dim) for p in sliced]
    sets = [sliced[0]]
    for k in range(1, outer):
        sets.append(swap(sliced[k], k * cores))
    for k in range(outer):
        sets.append(swap(sliced[k], k * cores + 1))

    group = steps * heads
    everything = rows * group
    stat = jax.ShapeDtypeStruct((everything, head_dim), float32)
    weight_half = jax.ShapeDtypeStruct((out_weight.shape[0], half), bfloat16)
    q_shape = jax.ShapeDtypeStruct((everything, head_dim), bfloat16)
    other_lanes = (pool_size - 1) * page_rows
    lanes = 2 * length + page_rows
    acc, top, total, q, owner, weight_send, weight_keep, own_residual = call(
        functools.partial(cache_kernel, scale),
        (
            stat, stat, stat, q_shape, jax.ShapeDtypeStruct((8, other_lanes), jnp.int32), weight_half, weight_half,
            jax.ShapeDtypeStruct((tokens, half), float32),
        ),
        [HBM] * 4 + [VMEM] + [HBM] * 3,
        scratch=[
            pltpu.VMEM((rows, length, 2, head_dim), bfloat16),
            pltpu.VMEM((rows, steps, half), bfloat16),
            pltpu.VMEM((everything, lanes), float32),
            pltpu.VMEM((everything, lanes), bfloat16),
            pltpu.SMEM((rows,), jnp.int32),
            pltpu.SMEM(page_row[:, 0].shape, jnp.int32),
            pltpu.SMEM(page_len[:, 0].shape, jnp.int32),
            pltpu.SemaphoreType.DMA((5,)),
            pltpu.SemaphoreType.DMA((rows,)),
            pltpu.SemaphoreType.DMA((2, 4)),
        ],
        vmem=24,
        flops=4 * everything * lanes * head_dim,
        bytes_accessed=kv_cache.size + out_weight.size * 2,
    )(
        far_off(cache_len), far_off(page_row[:, 0]), far_off(page_len[:, 0]),
        far_off(queries.reshape(everything, head_dim)), sets[0], far_off(kv_cache), far_off(out_weight),
        far_off(residual),
    )
    low, send = call(
        functools.partial(page_kernel, heads, rows, scale),
        (
            jax.ShapeDtypeStruct((tokens, heads * head_dim), bfloat16),
            jax.ShapeDtypeStruct((tokens, half), bfloat16),
        ),
        [VMEM] * (5 + pool_size),
        scratch=[
            pltpu.VMEM((everything, other_lanes), float32),
            pltpu.VMEM((everything, other_lanes), bfloat16),
            pltpu.VMEM((2, everything, head_dim), float32),
        ],
        flops=2 * tokens * heads * head_dim * half,
    )(q, acc, top, total, owner, *sets[1:], weight_send)
    arrived = swap(send, 1)
    keep = call(
        project_kernel, jax.ShapeDtypeStruct((tokens, half), float32), [VMEM] * 3,
        flops=2 * tokens * heads * head_dim * half,
    )(low, weight_keep, own_residual)

    experts = gate_weight.shape[0] * expert_size
    wide = -(-2 * experts // LANES) * LANES
    routes = routes.reshape(tokens, -1)
    named = routes[:, :, None] == jnp.arange(wide, dtype=jnp.int32) % experts
    table = jnp.sum(jnp.where(named, route_weight.reshape(tokens, -1, 1), 0.0), axis=1)
    coarse = lax.reduce_precision(table, 8, 7)
    table = jnp.where(jnp.arange(wide) < experts, coarse, jnp.where(jnp.arange(wide) < 2 * experts, table - coarse, 0.0))

    partial = keep + arrived.astype(float32)
    summed = partial.astype(bfloat16)
    hidden = summed.astype(float32)
    for k in range(1, outer):
        hidden = hidden + swap(summed, k * cores).astype(float32)
    message = jnp.concatenate([hidden, table], axis=1).astype(bfloat16)
    gate_near, up_near, down_near = gate_weight, up_weight, down_weight
    units = gate_weight.shape[0] * gate_weight.shape[2]
    result = 0.0
    flips = list(range(far - 1, 0, -1))
    same = [message]
    for k in flips:
        same.append(swap(message, 0, k * near))
    beside = swap(message, 0, 1)
    same = jnp.concatenate(same, axis=0)
    rest = swap(same[tokens:], 0, 1)
    gathered = (same, jnp.concatenate([beside, rest], axis=0))
    for index, own in enumerate(gathered):
        other = swap(own, 1)
        batch = [k * near + index for k in [0] + flips]
        here = len(batch) * tokens
        act, outgoing = call(
            expert_kernel,
            (jax.ShapeDtypeStruct((here, units), bfloat16), jax.ShapeDtypeStruct((here, half), bfloat16)),
            [VMEM] * 5,
            flops=5 * here * width * units,
        )(own, other, gate_near, up_near, down_near)
        incoming = swap(outgoing, 1)
        kept = call(
            down_kernel, jax.ShapeDtypeStruct((here, half), float32), [VMEM] * 2, flops=2 * here * half * units
        )(act, down_near)
        total = kept + incoming.astype(float32)
        for n, k in enumerate(batch):
            part = total[n * tokens : (n + 1) * tokens]
            if k:
                part = swap(part.astype(bfloat16), 0, k).astype(float32)
            result = result + part
    outcome = result.astype(bfloat16)
    result = hidden + result
    for k in range(1, outer):
        result = result + swap(outcome, k * cores).astype(float32)
    mine = result.astype(bfloat16)
    theirs = swap(mine, 1)
    return call(
        finish_kernel, jax.ShapeDtypeStruct(residual.shape, bfloat16), [VMEM] * 2, vmem=4, bytes_accessed=4 * residual.size
    )(mine, theirs)


def solution(mesh):
    return jax.shard_map(
        per_device,
        mesh=mesh,
        in_specs=(
            P("expert", None, None),
            P("expert", None, "pool", None),
            P("expert", None, None, None, None),
            P("pool", "expert", None, None, None, None),
            P("expert"),
            P(None, "expert"),
            P(None, "expert"),
            P("expert", None, None),
            P("expert", None, None),
            P("pool", None),
            P("expert", None, "pool"),
            P("expert", None, "pool"),
            P("expert", "pool", None),
        ),
        out_specs=P("expert", None, None),
        check_vma=False,
    )
```

```python
import functools
import math

import jax
import jax.numpy as jnp
from jax import lax
from jax.experimental import pallas as pl
from jax.experimental.pallas import tpu as pltpu
from jax.sharding import PartitionSpec as P


MIB = 1 << 20
LANES = 128
very_low = -1e30
cores = 2
near = 2
VMEM = pl.BlockSpec(memory_space=pltpu.VMEM)
HBM = pl.BlockSpec(memory_space=pltpu.HBM)
ANY = pl.BlockSpec(memory_space=pl.ANY)
float32 = jnp.float32
bfloat16 = jnp.bfloat16


def far_off(array):
    return pltpu.with_memory_space_constraint(array, pltpu.HBM)


def dot_t(a, b):
    return lax.dot_general(a, b, (((1,), (1,)), ((), ())), preferred_element_type=float32)


def dot(a, b):
    return jnp.dot(a, b, preferred_element_type=float32)


def slice_kernel(kv_heads, pages_hbm, own_ref, *rest):
    others, sem = rest[:-1], rest[-1]
    pool_size = lax.axis_size("pool")
    me = lax.axis_index("pool")
    copies = []
    for k, dest in enumerate((own_ref,) + others):
        head = (me ^ (k * cores)) * kv_heads // pool_size
        copies.append(pltpu.make_async_copy(pages_hbm.at[:, 0, :, head], dest, sem.at[k]))
    for copy in copies[::-1]:
        copy.start()
    for copy in copies:
        copy.wait()


def cache_kernel(
    scale, len_hbm, row_hbm, size_hbm, q_hbm, own_ref, kv_hbm, weight_hbm, residual_hbm,
    acc_ref, top_ref, total_ref, q_ref, owner_ref, weight_ref, residual_ref,
    kv_ref, raw_ref, score_ref, low_ref, len_ref, row_ref, size_ref, small_sem, kv_sem, weight_sem,
):
    rows, length, kv_heads = kv_hbm.shape[:3]
    head_dim = kv_hbm.shape[4]
    pool_size = lax.axis_size("pool")
    me = lax.axis_index("pool")
    core = me % cores
    head = me * kv_heads // pool_size
    small = [
        pltpu.make_async_copy(len_hbm, len_ref, small_sem.at[0]),
        pltpu.make_async_copy(row_hbm, row_ref, small_sem.at[1]),
        pltpu.make_async_copy(size_hbm, size_ref, small_sem.at[2]),
        pltpu.make_async_copy(q_hbm, q_ref, small_sem.at[3]),
    ]
    for copy in small:
        copy.start()
    copies = [pltpu.make_async_copy(kv_hbm.at[r, :, head], kv_ref.at[r], kv_sem.at[r]) for r in range(rows)]
    half = residual_ref.shape[1]
    mine = pl.ds(pl.multiple_of(core * half, half), half)
    chunks = weight_sem.shape[0]
    part = weight_hbm.shape[0] // chunks
    weights_in = [pltpu.make_async_copy(residual_hbm.at[:, :, mine], raw_ref, small_sem.at[4])]
    for n in range(chunks):
        rows_of = pl.ds(n * part, part)
        weights_in.append(pltpu.make_async_copy(weight_hbm.at[rows_of], weight_ref.at[rows_of], weight_sem.at[n]))
    for copy in weights_in + copies:
        copy.start()
    for copy in small:
        copy.wait()
    everything = q_ref.shape[0]
    group = everything // rows
    steps = residual_hbm.shape[1]
    deep = 2 * length
    kv_rows = kv_ref.reshape(rows, deep, head_dim)
    page_rows = own_ref.shape[0]
    held = row_ref.shape[0] // pool_size
    span = page_rows // held
    page_lane = lax.broadcasted_iota(jnp.int32, (8, span), 1)
    page_key = jnp.where(page_lane % 2 == 0, page_lane // 2, span)
    owners = []
    for k in range(pool_size):
        source = me ^ (k * cores if k * cores < pool_size else (k * cores) % pool_size + 1)
        for i in range(held):
            page = source * held + i
            owners.append(jnp.where(page_key < size_ref[page], row_ref[page], -1))
    owner_ref[...] = jnp.concatenate(owners[held:], axis=1)
    own_owner = jnp.concatenate(owners[:held], axis=1)[:1]
    lane = lax.broadcasted_iota(jnp.int32, (1, deep), 1)
    key = jnp.where(lane % 2 == 0, lane // 2, 2 * length)
    step = lax.broadcasted_iota(jnp.int32, (group, 1), 0) // (group // steps)
    score_ref[:, deep:] = dot_t(q_ref[...], own_ref[...])
    here = [slice(r * group, (r + 1) * group) for r in range(rows)]
    for r in range(rows):
        copies[r].wait()
        score_ref[here[r], :deep] = dot_t(q_ref[here[r], :], kv_rows[r])
    for r in range(rows):
        scores = score_ref[here[r], :] * scale
        seen = jnp.concatenate(
            [key <= len_ref[r] + step, jnp.broadcast_to(own_owner == r, (group, page_rows))], axis=1
        )
        scores = jnp.where(seen, scores, very_low)
        top = jnp.max(scores, axis=1, keepdims=True)
        weights = jnp.where(seen, jnp.exp(scores - top), 0.0)
        total = jnp.sum(weights, axis=1, keepdims=True)
        low_ref[here[r], :] = pltpu.roll(weights, 1, 1).astype(bfloat16)
        top_ref[here[r], :] = jnp.broadcast_to(top, (group, top_ref.shape[1]))
        total_ref[here[r], :] = jnp.broadcast_to(total, (group, total_ref.shape[1]))
    acc_ref[...] = dot(low_ref[:, deep:], own_ref[...])
    for r in range(rows):
        acc_ref[here[r], :] += dot(low_ref[here[r], :deep], kv_rows[r])
    for copy in weights_in:
        copy.wait()
    first = jnp.where(me // cores == 0, 1.0, 0.0)
    residual_ref[...] = raw_ref.reshape(*residual_ref.shape)[...].astype(float32) * first


def page_kernel(heads, rows, scale, q_ref, acc_in, top_in, total_in, owner_ref, *rest):
    pages = rest[:-6]
    weight_ref, low_ref, send_ref, score_ref, chance_ref, flat_ref = rest[-6:]
    everything, _ = q_ref.shape
    group = everything // rows
    size = pages[0].shape[0]
    for n, page in enumerate(pages):
        score_ref[:, n * size : (n + 1) * size] = dot_t(q_ref[...], page[...])
    owner = owner_ref[:1, :]
    for r in range(rows):
        here = slice(r * group, (r + 1) * group)
        seen = jnp.broadcast_to(owner == r, (group, owner.shape[1]))
        scores = jnp.where(seen, score_ref[here, :] * scale, very_low)
        top = jnp.maximum(top_in[here, :], jnp.max(scores, axis=1, keepdims=True))
        weights = jnp.where(seen, jnp.exp(scores - top[:, :1]), 0.0)
        shrink = jnp.exp(top_in[here, :] - top)
        total = total_in[here, :] * shrink + jnp.sum(weights, axis=1, keepdims=True)
        chance_ref[here, :] = pltpu.roll(weights, 1, 1).astype(bfloat16)
        inverse = 1.0 / total
        flat_ref[0, here, :] = inverse
        flat_ref[1, here, :] = acc_in[here, :] * shrink * inverse
    mixed = dot(chance_ref[:, :size], pages[0][...])
    for n in range(1, len(pages)):
        mixed = mixed + dot(chance_ref[:, n * size : (n + 1) * size], pages[n][...])
    flat_ref[1] = flat_ref[1] + mixed * flat_ref[0]
    tokens = everything // heads
    low = jnp.concatenate(
        [flat_ref[1, pl.ds(h, tokens, stride=heads), :].astype(bfloat16) for h in range(heads)], axis=1
    )
    low_ref[...] = low
    half = send_ref.shape[1]
    core = lax.axis_index("pool") % cores
    theirs = pl.ds(pl.multiple_of((1 - core) * half, half), half)
    send_ref[...] = dot(low, weight_ref[:, theirs]).astype(bfloat16)


def project_kernel(low_ref, weight_ref, residual_ref, keep_ref):
    half = keep_ref.shape[1]
    core = lax.axis_index("pool") % cores
    mine = pl.ds(pl.multiple_of(core * half, half), half)
    keep_ref[...] = dot(low_ref[...], weight_ref[:, mine]) + residual_ref[...]


def expert_kernel(own_ref, other_ref, gate_ref, up_ref, down_ref, act_ref, send_ref):
    half = send_ref.shape[1]
    own = own_ref[:, :half]
    other = other_ref[:, :half]
    table = own_ref[:, half:].astype(float32)
    lane = lax.broadcasted_iota(jnp.int32, table.shape, 1)
    core = lax.axis_index("pool") % cores
    first = pl.ds(pl.multiple_of(core * half, half), half)
    second = pl.ds(pl.multiple_of((1 - core) * half, half), half)
    experts, _, units = gate_ref.shape
    everyone = experts * lax.axis_size("expert")
    for j in range(experts):
        mine = lax.axis_index("expert") * experts + j
        weight = jnp.sum(
            jnp.where((lane == mine) | (lane == mine + everyone), table, 0.0), axis=1, keepdims=True
        )
        gate = dot(own, gate_ref[j, first, :]) + dot(other, gate_ref[j, second, :])
        up = dot(own, up_ref[j, first, :]) + dot(other, up_ref[j, second, :])
        active = gate / (1.0 + jnp.exp(-gate)) * up
        act_ref[:, j * units : (j + 1) * units] = (active * weight).astype(bfloat16)
    total = 0.0
    for j in range(experts):
        total = total + dot(act_ref[:, j * units : (j + 1) * units], down_ref[j, :, second])
    send_ref[...] = total.astype(bfloat16)


def down_kernel(act_ref, down_ref, keep_ref):
    half = keep_ref.shape[1]
    experts, units, _ = down_ref.shape
    core = lax.axis_index("pool") % cores
    first = pl.ds(pl.multiple_of(core * half, half), half)
    total = 0.0
    for j in range(experts):
        total = total + dot(act_ref[:, j * units : (j + 1) * units], down_ref[j, :, first])
    keep_ref[...] = total


def finish_kernel(mine_ref, theirs_ref, out_ref):
    tokens, half = mine_ref.shape
    core = lax.axis_index("pool") % cores
    flat = out_ref.reshape(tokens, out_ref.shape[2])
    flat[:, pl.ds(pl.multiple_of(core * half, half), half)] = mine_ref[...]
    flat[:, pl.ds(pl.multiple_of((1 - core) * half, half), half)] = theirs_ref[...]


def call(kernel, outs, specs, scratch=(), vmem=16, flops=0, bytes_accessed=0, **kw):
    return pl.pallas_call(
        kernel,
        out_shape=outs,
        in_specs=specs,
        out_specs=jax.tree.map(lambda _: VMEM, outs),
        scratch_shapes=scratch,
        compiler_params=pltpu.CompilerParams(vmem_limit_bytes=vmem * MIB),
        cost_estimate=pl.CostEstimate(flops=flops, bytes_accessed=bytes_accessed, transcendentals=0),
        **kw,
    )


def per_device(
    residual,
    queries,
    kv_cache,
    kv_pages,
    cache_len,
    page_row,
    page_len,
    routes,
    route_weight,
    out_weight,
    gate_weight,
    up_weight,
    down_weight,
):
    pool_size = lax.axis_size("pool")
    expert_size = lax.axis_size("expert")
    outer, far = pool_size // cores, expert_size // near

    def swap(value, pool_flip=0, expert_flip=0):
        pairs = []
        for p in range(pool_size):
            for e in range(expert_size):
                pairs.append((p * expert_size + e, (p ^ pool_flip) * expert_size + (e ^ expert_flip)))
        return lax.ppermute(value, ("pool", "expert"), pairs)

    rows, steps, heads, head_dim = queries.shape
    length, kv_heads = kv_cache.shape[1:3]
    held, _, page_size = kv_pages.shape[:3]
    width = residual.shape[2]
    half = width // cores
    tokens = rows * steps
    scale = 1.0 / math.sqrt(head_dim)

    page_rows = held * page_size * 2
    piece = jax.ShapeDtypeStruct((held, page_size, 2, head_dim), bfloat16)
    sliced = call(
        functools.partial(slice_kernel, kv_heads),
        (piece,) * outer,
        [HBM],
        scratch=[pltpu.SemaphoreType.DMA((outer,))],
        vmem=4,
        bytes_accessed=2 * kv_pages.size,
    )(far_off(kv_pages))
    sliced = [p.reshape(page_rows, head_dim) for p in sliced]
    sets = [sliced[0]]
    for k in range(1, outer):
        sets.append(swap(sliced[k], k * cores))
    for k in range(outer):
        sets.append(swap(sliced[k], k * cores + 1))

    group = steps * heads
    everything = rows * group
    stat = jax.ShapeDtypeStruct((everything, head_dim), float32)
    q_shape = jax.ShapeDtypeStruct((everything, head_dim), bfloat16)
    other_lanes = (pool_size - 1) * page_rows
    lanes = 2 * length + page_rows
    acc, top, total, q, owner, weight, own_residual = call(
        functools.partial(cache_kernel, scale),
        (
            stat, stat, stat, q_shape, jax.ShapeDtypeStruct((8, other_lanes), jnp.int32),
            jax.ShapeDtypeStruct(out_weight.shape, bfloat16),
            jax.ShapeDtypeStruct((tokens, half), float32),
        ),
        [HBM] * 4 + [VMEM] + [HBM] * 3,
        scratch=[
            pltpu.VMEM((rows, length, 2, head_dim), bfloat16),
            pltpu.VMEM((rows, steps, half), bfloat16),
            pltpu.VMEM((everything, lanes), float32),
            pltpu.VMEM((everything, lanes), bfloat16),
            pltpu.SMEM((rows,), jnp.int32),
            pltpu.SMEM(page_row[:, 0].shape, jnp.int32),
            pltpu.SMEM(page_len[:, 0].shape, jnp.int32),
            pltpu.SemaphoreType.DMA((5,)),
            pltpu.SemaphoreType.DMA((rows,)),
            pltpu.SemaphoreType.DMA((8,)),
        ],
        vmem=24,
        flops=4 * everything * lanes * head_dim,
        bytes_accessed=kv_cache.size + out_weight.size * 2,
    )(
        far_off(cache_len), far_off(page_row[:, 0]), far_off(page_len[:, 0]),
        far_off(queries.reshape(everything, head_dim)), sets[0], far_off(kv_cache), far_off(out_weight),
        far_off(residual),
    )
    low, send = call(
        functools.partial(page_kernel, heads, rows, scale),
        (
            jax.ShapeDtypeStruct((tokens, heads * head_dim), bfloat16),
            jax.ShapeDtypeStruct((tokens, half), bfloat16),
        ),
        [VMEM] * (5 + pool_size),
        scratch=[
            pltpu.VMEM((everything, other_lanes), float32),
            pltpu.VMEM((everything, other_lanes), bfloat16),
            pltpu.VMEM((2, everything, head_dim), float32),
        ],
        flops=2 * tokens * heads * head_dim * half,
    )(q, acc, top, total, owner, *sets[1:], weight)
    arrived = swap(send, 1)
    keep = call(
        project_kernel, jax.ShapeDtypeStruct((tokens, half), float32), [VMEM] * 3,
        flops=2 * tokens * heads * head_dim * half,
    )(low, weight, own_residual)

    experts = gate_weight.shape[0] * expert_size
    wide = -(-2 * experts // LANES) * LANES
    routes = routes.reshape(tokens, -1)
    named = routes[:, :, None] == jnp.arange(wide, dtype=jnp.int32) % experts
    table = jnp.sum(jnp.where(named, route_weight.reshape(tokens, -1, 1), 0.0), axis=1)
    coarse = lax.reduce_precision(table, 8, 7)
    table = jnp.where(jnp.arange(wide) < experts, coarse, jnp.where(jnp.arange(wide) < 2 * experts, table - coarse, 0.0))

    partial = keep + arrived.astype(float32)
    summed = partial.astype(bfloat16)
    hidden = summed.astype(float32)
    for k in range(1, outer):
        hidden = hidden + swap(summed, k * cores).astype(float32)
    message = jnp.concatenate([hidden, table], axis=1).astype(bfloat16)
    gate_near, up_near, down_near = gate_weight, up_weight, down_weight
    units = gate_weight.shape[0] * gate_weight.shape[2]
    result = 0.0
    flips = list(range(far - 1, 0, -1))
    same = [message]
    for k in flips:
        same.append(swap(message, 0, k * near))
    beside = swap(message, 0, 1)
    same = jnp.concatenate(same, axis=0)
    rest = swap(same[tokens:], 0, 1)
    gathered = (same, jnp.concatenate([beside, rest], axis=0))
    for index, own in enumerate(gathered):
        other = swap(own, 1)
        batch = [k * near + index for k in [0] + flips]
        here = len(batch) * tokens
        act, outgoing = call(
            expert_kernel,
            (jax.ShapeDtypeStruct((here, units), bfloat16), jax.ShapeDtypeStruct((here, half), bfloat16)),
            [VMEM] * 5,
            flops=5 * here * width * units,
        )(own, other, gate_near, up_near, down_near)
        incoming = swap(outgoing, 1)
        kept = call(
            down_kernel, jax.ShapeDtypeStruct((here, half), float32), [VMEM] * 2, flops=2 * here * half * units
        )(act, down_near)
        total = kept + incoming.astype(float32)
        for n, k in enumerate(batch):
            part = total[n * tokens : (n + 1) * tokens]
            if k:
                part = swap(part.astype(bfloat16), 0, k).astype(float32)
            result = result + part
    outcome = result.astype(bfloat16)
    result = hidden + result
    for k in range(1, outer):
        result = result + swap(outcome, k * cores).astype(float32)
    mine = result.astype(bfloat16)
    theirs = swap(mine, 1)
    return call(
        finish_kernel, jax.ShapeDtypeStruct(residual.shape, bfloat16), [VMEM] * 2, vmem=4, bytes_accessed=4 * residual.size
    )(mine, theirs)


def solution(mesh):
    return jax.shard_map(
        per_device,
        mesh=mesh,
        in_specs=(
            P("expert", None, None),
            P("expert", None, "pool", None),
            P("expert", None, None, None, None),
            P("pool", "expert", None, None, None, None),
            P("expert"),
            P(None, "expert"),
            P(None, "expert"),
            P("expert", None, None),
            P("expert", None, None),
            P("pool", None),
            P("expert", None, "pool"),
            P("expert", None, "pool"),
            P("expert", "pool", None),
        ),
        out_specs=P("expert", None, None),
        check_vma=False,
    )
```

```python
import functools
import math

import jax
import jax.numpy as jnp
from jax import lax
from jax.experimental import pallas as pl
from jax.experimental.pallas import tpu as pltpu
from jax.sharding import PartitionSpec as P


MIB = 1 << 20
LANES = 128
very_low = -1e30
cores = 2
near = 2
VMEM = pl.BlockSpec(memory_space=pltpu.VMEM)
HBM = pl.BlockSpec(memory_space=pltpu.HBM)
ANY = pl.BlockSpec(memory_space=pl.ANY)
float32 = jnp.float32
bfloat16 = jnp.bfloat16


def far_off(array):
    return pltpu.with_memory_space_constraint(array, pltpu.HBM)


def dot_t(a, b):
    return lax.dot_general(a, b, (((1,), (1,)), ((), ())), preferred_element_type=float32)


def dot(a, b):
    return jnp.dot(a, b, preferred_element_type=float32)


def slice_kernel(kv_heads, pages_hbm, own_ref, *rest):
    others, sem = rest[:-1], rest[-1]
    pool_size = lax.axis_size("pool")
    me = lax.axis_index("pool")
    copies = []
    for k, dest in enumerate((own_ref,) + others):
        head = (me ^ (k * cores)) * kv_heads // pool_size
        copies.append(pltpu.make_async_copy(pages_hbm.at[:, 0, :, head], dest, sem.at[k]))
    for copy in copies[::-1]:
        copy.start()
    for copy in copies:
        copy.wait()


def cache_kernel(
    scale, len_hbm, row_hbm, size_hbm, q_hbm, own_ref, kv_hbm, weight_hbm, residual_hbm,
    acc_ref, top_ref, total_ref, q_ref, owner_ref, weight_ref, residual_ref,
    kv_ref, raw_ref, score_ref, low_ref, len_ref, row_ref, size_ref, small_sem, kv_sem, weight_sem,
):
    rows, length, kv_heads = kv_hbm.shape[:3]
    head_dim = kv_hbm.shape[4]
    pool_size = lax.axis_size("pool")
    me = lax.axis_index("pool")
    core = me % cores
    head = me * kv_heads // pool_size
    small = [
        pltpu.make_async_copy(len_hbm, len_ref, small_sem.at[0]),
        pltpu.make_async_copy(row_hbm, row_ref, small_sem.at[1]),
        pltpu.make_async_copy(size_hbm, size_ref, small_sem.at[2]),
        pltpu.make_async_copy(q_hbm, q_ref, small_sem.at[3]),
    ]
    for copy in small:
        copy.start()
    copies = [pltpu.make_async_copy(kv_hbm.at[r, :, head], kv_ref.at[r], kv_sem.at[r]) for r in range(rows)]
    half = residual_ref.shape[1]
    mine = pl.ds(pl.multiple_of(core * half, half), half)
    chunks = weight_sem.shape[0]
    part = weight_hbm.shape[0] // chunks
    weights_in = [pltpu.make_async_copy(residual_hbm.at[:, :, mine], raw_ref, small_sem.at[4])]
    for n in range(chunks):
        rows_of = pl.ds(n * part, part)
        weights_in.append(pltpu.make_async_copy(weight_hbm.at[rows_of], weight_ref.at[rows_of], weight_sem.at[n]))
    for copy in weights_in + copies:
        copy.start()
    for copy in small:
        copy.wait()
    everything = q_ref.shape[0]
    group = everything // rows
    steps = residual_hbm.shape[1]
    deep = 2 * length
    kv_rows = kv_ref.reshape(rows, deep, head_dim)
    page_rows = own_ref.shape[0]
    held = row_ref.shape[0] // pool_size
    span = page_rows // held
    page_lane = lax.broadcasted_iota(jnp.int32, (8, span), 1)
    page_key = jnp.where(page_lane % 2 == 0, page_lane // 2, span)
    owners = []
    for k in range(pool_size):
        source = me ^ (k * cores if k * cores < pool_size else (k * cores) % pool_size + 1)
        for i in range(held):
            page = source * held + i
            owners.append(jnp.where(page_key < size_ref[page], row_ref[page], -1))
    owner_ref[...] = jnp.concatenate(owners[held:], axis=1)
    own_owner = jnp.concatenate(owners[:held], axis=1)[:1]
    lane = lax.broadcasted_iota(jnp.int32, (1, deep), 1)
    key = jnp.where(lane % 2 == 0, lane // 2, 2 * length)
    step = lax.broadcasted_iota(jnp.int32, (group, 1), 0) // (group // steps)
    score_ref[:, deep:] = dot_t(q_ref[...], own_ref[...])
    here = [slice(r * group, (r + 1) * group) for r in range(rows)]
    for r in range(rows):
        copies[r].wait()
        score_ref[here[r], :deep] = dot_t(q_ref[here[r], :], kv_rows[r])
    for r in range(rows):
        scores = score_ref[here[r], :] * scale
        seen = jnp.concatenate(
            [key <= len_ref[r] + step, jnp.broadcast_to(own_owner == r, (group, page_rows))], axis=1
        )
        scores = jnp.where(seen, scores, very_low)
        top = jnp.max(scores, axis=1, keepdims=True)
        weights = jnp.where(seen, jnp.exp(scores - top), 0.0)
        total = jnp.sum(weights, axis=1, keepdims=True)
        low_ref[here[r], :] = pltpu.roll(weights, 1, 1).astype(bfloat16)
        top_ref[here[r], :] = jnp.broadcast_to(top, (group, top_ref.shape[1]))
        total_ref[here[r], :] = jnp.broadcast_to(total, (group, total_ref.shape[1]))
    acc_ref[...] = dot(low_ref[:, deep:], own_ref[...])
    for r in range(rows):
        acc_ref[here[r], :] += dot(low_ref[here[r], :deep], kv_rows[r])
    for copy in weights_in:
        copy.wait()
    first = jnp.where(me // cores == 0, 1.0, 0.0)
    residual_ref[...] = raw_ref.reshape(*residual_ref.shape)[...].astype(float32) * first


def page_kernel(heads, rows, scale, q_ref, acc_in, top_in, total_in, owner_ref, *rest):
    pages = rest[:-6]
    weight_ref, low_ref, send_ref, score_ref, chance_ref, flat_ref = rest[-6:]
    everything, _ = q_ref.shape
    group = everything // rows
    size = pages[0].shape[0]
    for n, page in enumerate(pages):
        score_ref[:, n * size : (n + 1) * size] = dot_t(q_ref[...], page[...])
    owner = owner_ref[:1, :]
    for r in range(rows):
        here = slice(r * group, (r + 1) * group)
        seen = jnp.broadcast_to(owner == r, (group, owner.shape[1]))
        scores = jnp.where(seen, score_ref[here, :] * scale, very_low)
        top = jnp.maximum(top_in[here, :], jnp.max(scores, axis=1, keepdims=True))
        weights = jnp.where(seen, jnp.exp(scores - top[:, :1]), 0.0)
        shrink = jnp.exp(top_in[here, :] - top)
        total = total_in[here, :] * shrink + jnp.sum(weights, axis=1, keepdims=True)
        chance_ref[here, :] = pltpu.roll(weights, 1, 1).astype(bfloat16)
        inverse = 1.0 / total
        flat_ref[0, here, :] = inverse
        flat_ref[1, here, :] = acc_in[here, :] * shrink * inverse
    mixed = dot(chance_ref[:, :size], pages[0][...])
    for n in range(1, len(pages)):
        mixed = mixed + dot(chance_ref[:, n * size : (n + 1) * size], pages[n][...])
    flat_ref[1] = flat_ref[1] + mixed * flat_ref[0]
    tokens = everything // heads
    low = jnp.concatenate(
        [flat_ref[1, pl.ds(h, tokens, stride=heads), :].astype(bfloat16) for h in range(heads)], axis=1
    )
    low_ref[...] = low
    half = send_ref.shape[1]
    core = lax.axis_index("pool") % cores
    theirs = pl.ds(pl.multiple_of((1 - core) * half, half), half)
    send_ref[...] = dot(low, weight_ref[:, theirs]).astype(bfloat16)


def project_kernel(low_ref, weight_ref, residual_ref, keep_ref):
    half = keep_ref.shape[1]
    core = lax.axis_index("pool") % cores
    mine = pl.ds(pl.multiple_of(core * half, half), half)
    keep_ref[...] = dot(low_ref[...], weight_ref[:, mine]) + residual_ref[...]


def expert_kernel(own_ref, other_ref, gate_ref, up_ref, down_ref, act_ref, send_ref):
    half = send_ref.shape[1]
    own = own_ref[:, :half]
    other = other_ref[:, :half]
    table = own_ref[:, half:].astype(float32)
    lane = lax.broadcasted_iota(jnp.int32, table.shape, 1)
    core = lax.axis_index("pool") % cores
    first = pl.ds(pl.multiple_of(core * half, half), half)
    second = pl.ds(pl.multiple_of((1 - core) * half, half), half)
    experts, _, units = gate_ref.shape
    everyone = experts * lax.axis_size("expert")
    for j in range(experts):
        mine = lax.axis_index("expert") * experts + j
        weight = jnp.sum(
            jnp.where((lane == mine) | (lane == mine + everyone), table, 0.0), axis=1, keepdims=True
        )
        gate = dot(own, gate_ref[j, first, :]) + dot(other, gate_ref[j, second, :])
        up = dot(own, up_ref[j, first, :]) + dot(other, up_ref[j, second, :])
        active = gate / (1.0 + jnp.exp(-gate)) * up
        act_ref[:, j * units : (j + 1) * units] = (active * weight).astype(bfloat16)
    total = 0.0
    for j in range(experts):
        total = total + dot(act_ref[:, j * units : (j + 1) * units], down_ref[j, :, second])
    send_ref[...] = total.astype(bfloat16)


def down_kernel(act_ref, down_ref, keep_ref):
    half = keep_ref.shape[1]
    experts, units, _ = down_ref.shape
    core = lax.axis_index("pool") % cores
    first = pl.ds(pl.multiple_of(core * half, half), half)
    total = 0.0
    for j in range(experts):
        total = total + dot(act_ref[:, j * units : (j + 1) * units], down_ref[j, :, first])
    keep_ref[...] = total


def finish_kernel(mine_ref, theirs_ref, out_ref):
    tokens, half = mine_ref.shape
    core = lax.axis_index("pool") % cores
    flat = out_ref.reshape(tokens, out_ref.shape[2])
    flat[:, pl.ds(pl.multiple_of(core * half, half), half)] = mine_ref[...]
    flat[:, pl.ds(pl.multiple_of((1 - core) * half, half), half)] = theirs_ref[...]


def call(kernel, outs, specs, scratch=(), vmem=16, flops=0, bytes_accessed=0, **kw):
    return pl.pallas_call(
        kernel,
        out_shape=outs,
        in_specs=specs,
        out_specs=jax.tree.map(lambda _: VMEM, outs),
        scratch_shapes=scratch,
        compiler_params=pltpu.CompilerParams(vmem_limit_bytes=vmem * MIB),
        cost_estimate=pl.CostEstimate(flops=flops, bytes_accessed=bytes_accessed, transcendentals=0),
        **kw,
    )


def per_device(
    residual,
    queries,
    kv_cache,
    kv_pages,
    cache_len,
    page_row,
    page_len,
    routes,
    route_weight,
    out_weight,
    gate_weight,
    up_weight,
    down_weight,
):
    pool_size = lax.axis_size("pool")
    expert_size = lax.axis_size("expert")
    outer, far = pool_size // cores, expert_size // near

    def swap(value, pool_flip=0, expert_flip=0):
        pairs = []
        for p in range(pool_size):
            for e in range(expert_size):
                pairs.append((p * expert_size + e, (p ^ pool_flip) * expert_size + (e ^ expert_flip)))
        return lax.ppermute(value, ("pool", "expert"), pairs)

    rows, steps, heads, head_dim = queries.shape
    length, kv_heads = kv_cache.shape[1:3]
    held, _, page_size = kv_pages.shape[:3]
    width = residual.shape[2]
    half = width // cores
    tokens = rows * steps
    scale = 1.0 / math.sqrt(head_dim)

    page_rows = held * page_size * 2
    piece = jax.ShapeDtypeStruct((held, page_size, 2, head_dim), bfloat16)
    sliced = call(
        functools.partial(slice_kernel, kv_heads),
        (piece,) * outer,
        [HBM],
        scratch=[pltpu.SemaphoreType.DMA((outer,))],
        vmem=4,
        bytes_accessed=2 * kv_pages.size,
    )(far_off(kv_pages))
    sliced = [p.reshape(page_rows, head_dim) for p in sliced]
    sets = [sliced[0]]
    for k in range(1, outer):
        sets.append(swap(sliced[k], k * cores))
    for k in range(outer):
        sets.append(swap(sliced[k], k * cores + 1))

    group = steps * heads
    everything = rows * group
    stat = jax.ShapeDtypeStruct((everything, head_dim), float32)
    q_shape = jax.ShapeDtypeStruct((everything, head_dim), bfloat16)
    other_lanes = (pool_size - 1) * page_rows
    lanes = 2 * length + page_rows
    acc, top, total, q, owner, weight, own_residual = call(
        functools.partial(cache_kernel, scale),
        (
            stat, stat, stat, q_shape, jax.ShapeDtypeStruct((8, other_lanes), jnp.int32),
            jax.ShapeDtypeStruct(out_weight.shape, bfloat16),
            jax.ShapeDtypeStruct((tokens, half), float32),
        ),
        [HBM] * 4 + [VMEM] + [HBM] * 3,
        scratch=[
            pltpu.VMEM((rows, length, 2, head_dim), bfloat16),
            pltpu.VMEM((rows, steps, half), bfloat16),
            pltpu.VMEM((everything, lanes), float32),
            pltpu.VMEM((everything, lanes), bfloat16),
            pltpu.SMEM((rows,), jnp.int32),
            pltpu.SMEM(page_row[:, 0].shape, jnp.int32),
            pltpu.SMEM(page_len[:, 0].shape, jnp.int32),
            pltpu.SemaphoreType.DMA((5,)),
            pltpu.SemaphoreType.DMA((rows,)),
            pltpu.SemaphoreType.DMA((8,)),
        ],
        vmem=24,
        flops=4 * everything * lanes * head_dim,
        bytes_accessed=kv_cache.size + out_weight.size * 2,
    )(
        far_off(cache_len), far_off(page_row[:, 0]), far_off(page_len[:, 0]),
        far_off(queries.reshape(everything, head_dim)), sets[0], far_off(kv_cache), far_off(out_weight),
        far_off(residual),
    )
    low, send = call(
        functools.partial(page_kernel, heads, rows, scale),
        (
            jax.ShapeDtypeStruct((tokens, heads * head_dim), bfloat16),
            jax.ShapeDtypeStruct((tokens, half), bfloat16),
        ),
        [VMEM] * (5 + pool_size),
        scratch=[
            pltpu.VMEM((everything, other_lanes), float32),
            pltpu.VMEM((everything, other_lanes), bfloat16),
            pltpu.VMEM((2, everything, head_dim), float32),
        ],
        flops=2 * tokens * heads * head_dim * half,
    )(q, acc, top, total, owner, *sets[1:], weight)
    arrived = swap(send, 1)
    keep = call(
        project_kernel, jax.ShapeDtypeStruct((tokens, half), float32), [VMEM] * 3,
        flops=2 * tokens * heads * head_dim * half,
    )(low, weight, own_residual)

    experts = gate_weight.shape[0] * expert_size
    wide = -(-2 * experts // LANES) * LANES
    routes = routes.reshape(tokens, -1)
    named = routes[:, :, None] == jnp.arange(wide, dtype=jnp.int32) % experts
    table = jnp.sum(jnp.where(named, route_weight.reshape(tokens, -1, 1), 0.0), axis=1)
    coarse = lax.reduce_precision(table, 8, 7)
    table = jnp.where(jnp.arange(wide) < experts, coarse, jnp.where(jnp.arange(wide) < 2 * experts, table - coarse, 0.0))

    partial = keep + arrived.astype(float32)
    summed = partial.astype(bfloat16)
    hidden = summed.astype(float32)
    for k in range(1, outer):
        hidden = hidden + swap(summed, k * cores).astype(float32)
    message = jnp.concatenate([hidden, table], axis=1).astype(bfloat16)
    gate_near, up_near, down_near = gate_weight, up_weight, down_weight
    units = gate_weight.shape[0] * gate_weight.shape[2]
    first = jnp.where(lax.axis_index("pool") // cores == 0, 1.0, 0.0)
    result = 0.0
    flips = list(range(far - 1, 0, -1))
    same = [message]
    for k in flips:
        same.append(swap(message, 0, k * near))
    beside = swap(message, 0, 1)
    same = jnp.concatenate(same, axis=0)
    rest = swap(same[tokens:], 0, 1)
    gathered = (same, jnp.concatenate([beside, rest], axis=0))
    for index, own in enumerate(gathered):
        other = swap(own, 1)
        batch = [k * near + index for k in [0] + flips]
        here = len(batch) * tokens
        act, outgoing = call(
            expert_kernel,
            (jax.ShapeDtypeStruct((here, units), bfloat16), jax.ShapeDtypeStruct((here, half), bfloat16)),
            [VMEM] * 5,
            flops=5 * here * width * units,
        )(own, other, gate_near, up_near, down_near)
        incoming = swap(outgoing, 1)
        kept = call(
            down_kernel, jax.ShapeDtypeStruct((here, half), float32), [VMEM] * 2, flops=2 * here * half * units
        )(act, down_near)
        total = kept + incoming.astype(float32)
        for n, k in enumerate(batch):
            part = total[n * tokens : (n + 1) * tokens]
            if k:
                part = swap(part.astype(bfloat16), 0, k).astype(float32)
            result = result + part
    outcome = result.astype(bfloat16)
    shared = (result + hidden * first).astype(bfloat16)
    mine = result + hidden
    for k in range(1, outer):
        mine = mine + swap(outcome, k * cores).astype(float32)
    theirs = 0.0
    for k in range(outer - 1, -1, -1):
        theirs = theirs + swap(shared, k * cores + 1).astype(float32)
    mine, theirs = mine.astype(bfloat16), theirs.astype(bfloat16)
    return call(
        finish_kernel, jax.ShapeDtypeStruct(residual.shape, bfloat16), [VMEM] * 2, vmem=4, bytes_accessed=4 * residual.size
    )(mine, theirs)


def solution(mesh):
    return jax.shard_map(
        per_device,
        mesh=mesh,
        in_specs=(
            P("expert", None, None),
            P("expert", None, "pool", None),
            P("expert", None, None, None, None),
            P("pool", "expert", None, None, None, None),
            P("expert"),
            P(None, "expert"),
            P(None, "expert"),
            P("expert", None, None),
            P("expert", None, None),
            P("pool", None),
            P("expert", None, "pool"),
            P("expert", None, "pool"),
            P("expert", "pool", None),
        ),
        out_specs=P("expert", None, None),
        check_vma=False,
    )
```
